1024 devices in a mesh: fsdp: 16 (over y, core), tile: 64 (over x, z).
Axes of the slice: x: 4, y: 8, z: 16, core: 2. Of those that a mesh axis runs over, the one named last changes fastest.
Arguments:
- tiles: bfloat16 [16, 16384, 768], P('fsdp', 'tile')
- nbr_tiles: int32 [16, 4096, 4], P('fsdp', 'tile'), may hold values from 0 to 16383, as said below
- nbr_mask: int32 [16, 4096, 4], P('fsdp', 'tile'), may hold values 0 or 1
- tile_count: int32 [16], P('fsdp'), may hold values from 8192 to 16384, as said below
- w_query: bfloat16 [768, 768], P('fsdp'), may hold values from -0.21875 to 0.21875
- w_key: bfloat16 [768, 768], P('fsdp'), may hold values from -0.21875 to 0.21875
- w_value: bfloat16 [768, 768], P('fsdp'), may hold values from -0.21875 to 0.21875
- w_out: bfloat16 [768, 768], P('fsdp'), may hold values from -0.875 to 0.875
- key_gain: float32 [768], replicated, may hold values from 0.1 to 1.9
Outputs:
- attended: bfloat16 [16, 16384, 768], P('fsdp', 'tile')
The draws below stay inside these ranges and needn't reach their ends.
Inputs may be any that keep to these rules, and one draw needn't show every extreme that they name: `nbr_tiles`: the slots of region r hold tiles with indices from (r // 64 - 1) * 256 to (r // 64 + 2) * 256 - 1, within the group. `tile_count`: some group has all 16384 tiles live.
All inputs are finite; a program needn't handle non-finite values. No bound on the sum of `nbr_mask` on one device may be relied on, other than what follows from the above.
Results may differ from the reference program's by a relative error of at most 0.008.
The reference program's roundings to bfloat16 on the way (of `normed`, `weight` and `context`) count: a program that leaves them out, or rounds other values in their place, can miss the bound.
Values may be sent and summed in bfloat16 or wider, within the bound.
A program may use at most 32 MiB of HBM per device.

```python
import jax
import jax.numpy as jnp
from jax import lax

D = 768
HEADS = 16
TILE_DEV = 256
NB = 4
REGIONS_PER_KEY = 8
KEY_DILATION = 2
HD = 48
GROUPS = 16
TILES = 16384
REGIONS = 4096
KEYS = 512


def draw_tiles(key, part):
    base = jax.random.normal(jax.random.fold_in(key, 1), (GROUPS, TILES, D), jnp.float32)
    return base.astype(jnp.bfloat16)


def draw_nbr_tiles(key, part):
    owner = jnp.arange(REGIONS, dtype=jnp.int32) // (TILE_DEV // 4)
    offset = jax.random.randint(jax.random.fold_in(key, 5), (GROUPS, REGIONS, NB), -TILE_DEV, 2 * TILE_DEV, dtype=jnp.int32)
    return jnp.clip(owner[None, :, None] * TILE_DEV + offset, 0, TILES - 1).astype(jnp.int32)


def draw_tile_count(key, part):
    counts = jax.random.randint(jax.random.fold_in(key, 6), (GROUPS,), TILES // 2, TILES + 1, dtype=jnp.int32)
    selected_keys = jax.random.randint(jax.random.fold_in(key, 7), (), 0, GROUPS, dtype=jnp.int32)
    return jnp.where(jnp.arange(GROUPS, dtype=jnp.int32) == selected_keys, TILES, counts).astype(jnp.int32)


def with_ends(entries, key, low, top_value):
    dims = entries.shape
    place = [jax.random.randint(jax.random.fold_in(key, axis), (), 0, dims[axis]) for axis in range(len(dims))]
    entries = entries.at[tuple(place)].set(low)
    longest = dims.index(max(dims))
    place[longest] = (place[longest] + 1) % dims[longest]
    return entries.at[tuple(place)].set(top_value)


def block_scale(own_key, extent, split, smallest, top_value):
    def one(axis_at, blocks):
        steps = jax.random.uniform(jax.random.fold_in(jax.random.fold_in(own_key, 6), axis_at), (blocks,), jnp.float32, smallest / len(split), top_value / len(split))
        return jnp.repeat(jnp.exp(steps), extent[axis_at] // blocks).reshape((-1,) + (1,) * (len(extent) - axis_at - 1))

    loudness = one(*split[0])
    for cut in split[1:]:
        loudness = loudness * one(*cut)
    return loudness


def scatter_about(stream_key, extent, spread, limit, split=(), held_as=jnp.bfloat16):
    level = block_scale(stream_key, extent, split, -0.22, 0.18) if split else 1.0
    array = jax.random.normal(stream_key, extent, jnp.float32) * spread * level
    return jnp.minimum(jnp.maximum(array, -limit), limit).astype(held_as)


def setup_inputs(seed: int = 0) -> dict:
    splits = jax.random.split(jax.random.key(seed), 10)
    tiles = draw_tiles(jax.random.fold_in(splits[9], 71), 0)
    nbr_tiles = draw_nbr_tiles(jax.random.fold_in(splits[9], 71), 0)
    nbr_mask = with_ends((jax.random.randint(splits[2], (GROUPS, REGIONS, NB), 0, 4) < 3).astype(jnp.int32), jax.random.fold_in(splits[2], 1), 0, 1)
    tile_count = draw_tile_count(jax.random.fold_in(splits[9], 71), 0)
    w_query = scatter_about(splits[4], (D, D), D ** -0.5, 0.21875, ((0, 16),))
    w_key = scatter_about(splits[5], (D, D), D ** -0.5, 0.21875, ((0, 16),))
    w_value = scatter_about(splits[6], (D, D), D ** -0.5, 0.21875, ((0, 16),))
    w_out = scatter_about(splits[7], (D, D), HD ** -0.5, 0.875, ((0, 16),))
    key_gain = jnp.clip(1.0 + 0.18 * jax.random.normal(splits[8], (D,), jnp.float32), 0.1, 1.9)
    return dict(tiles=tiles, nbr_tiles=nbr_tiles, nbr_mask=nbr_mask, tile_count=tile_count, w_query=w_query, w_key=w_key, w_value=w_value, w_out=w_out, key_gain=key_gain)


def one_group(args):
    tiles, nbr_tiles, nbr_mask, key_count_total, w_query, w_key, w_value, w_out, key_gain = args
    rows = tiles.astype(jnp.float32)[nbr_tiles.reshape(-1)].reshape(REGIONS, NB, D)
    mask_f = nbr_mask.astype(jnp.float32)
    denom = jnp.maximum(lax.optimization_barrier(jnp.sum(mask_f, axis=1)), 1.0)
    region = lax.optimization_barrier(jnp.sum(rows * mask_f[:, :, None], axis=1)) / denom[:, None]
    pooled = lax.optimization_barrier(jnp.mean(region.reshape(KEYS, REGIONS_PER_KEY, D), axis=1))
    normed = (pooled * lax.rsqrt(lax.optimization_barrier(jnp.mean(pooled * pooled, axis=1, keepdims=True)) + 1e-06) * key_gain[None, :]).astype(jnp.bfloat16)
    keys = jnp.dot(normed, w_key, preferred_element_type=jnp.float32).astype(jnp.bfloat16)
    values = jnp.dot(normed, w_value, preferred_element_type=jnp.float32).astype(jnp.bfloat16)
    key_heads = keys.astype(jnp.float32).reshape(KEYS, HEADS, HD)
    value_heads = values.astype(jnp.float32).reshape(KEYS, HEADS, HD)
    key_position = jnp.arange(KEYS, dtype=jnp.int32)
    head_position = jnp.arange(HEADS, dtype=jnp.int32)
    valid_mask = ((key_position % KEY_DILATION)[None, :] == (head_position % KEY_DILATION)[:, None]) & (key_position * 4 * REGIONS_PER_KEY < key_count_total)[None, :]
    block = min(2048, TILES)

    def attend(tile_block):
        query = jnp.dot(tile_block, w_query, preferred_element_type=jnp.float32).astype(jnp.bfloat16)
        query_heads = query.astype(jnp.float32).reshape(-1, HEADS, HD)
        score = jnp.einsum('qhd,khd->hqk', query_heads, key_heads) / jnp.sqrt(jnp.float32(HD))
        score = jnp.where(valid_mask[:, None, :], score, -jnp.inf)
        top = lax.optimization_barrier(jnp.max(score, axis=2, keepdims=True))
        expo = jnp.exp(score - top)
        total = lax.optimization_barrier(jnp.sum(expo, axis=2))
        weight = expo.astype(jnp.bfloat16).astype(jnp.float32)
        context = jnp.einsum('hqk,khd->hqd', weight, value_heads) / total[:, :, None]
        context = jnp.transpose(context, (1, 0, 2)).reshape(-1, D).astype(jnp.bfloat16)
        return jnp.dot(context, w_out, preferred_element_type=jnp.float32).astype(jnp.bfloat16)
    out = lax.map(attend, tiles.reshape(TILES // block, block, D))
    return out.reshape(TILES, D)

def reference(tiles, nbr_tiles, nbr_mask, tile_count, w_query, w_key, w_value, w_out, key_gain):
    outs = []
    for group in range(GROUPS):
        outs.append(one_group((tiles[group], nbr_tiles[group], nbr_mask[group], tile_count[group], w_query, w_key, w_value, w_out, key_gain)))
    return jnp.stack(outs, axis=0)
```

```python
import functools
import math

import jax
import jax.numpy as jnp
from jax import lax
from jax.experimental import pallas as pl
from jax.experimental.pallas import tpu as pltpu
from jax.sharding import PartitionSpec as P

HEADS = 16
REGIONS_PER_KEY = 8
TILES_PER_KEY = 32
NZ = 16
MESH = pl.DeviceIdType.MESH
BF16 = jnp.bfloat16
F32 = jnp.float32
WINDOWS = ((0, 128), (0, 128), (0, 256), (128, 128), (128, 128), (128, 256), (256, 128), (256, 128))


def pooling_weights(idx, msk, base, rows):
    m = msk.astype(F32)
    share = m / jnp.maximum(jnp.sum(m, axis=0, keepdims=True), 1.0)
    at = idx - base
    slots, regions = idx.shape
    tile = lax.broadcasted_iota(jnp.int32, (rows, regions), 0)
    acc = jnp.zeros((rows, regions), F32)
    for s in range(slots):
        acc = acc + jnp.where(tile == at[s : s + 1, :], share[s : s + 1, :], 0.0)
    acc = acc.T
    keys = regions // REGIONS_PER_KEY
    return jnp.sum(acc.reshape(keys, REGIONS_PER_KEY, rows), axis=1) * (1.0 / REGIONS_PER_KEY)


def exact_dot(w, x):
    hi = w.astype(BF16)
    rest = w - hi.astype(F32)
    mid = rest.astype(BF16)
    low = (rest - mid.astype(F32)).astype(BF16)
    n = w.shape[0]
    parts = jnp.concatenate([hi.astype(F32), mid.astype(F32), low.astype(F32)], axis=0).astype(BF16)
    y = jnp.dot(parts, x, preferred_element_type=F32)
    return y[:n] + y[n : 2 * n] + y[2 * n :]


def kernel(
    ny, nx, nz,
    tiles_hbm, idx_ref, msk_ref, cnt_ref, wq_hbm, wk_hbm, wv_hbm, wo_hbm, gain_ref,
    out_ref,
    tiles_v, w_v, ng, nf, nidx, nmsk, pout, pin, qz, kk, vt, ctxt, wvt,
    loc_sem, halo_send, halo_recv, ring_send, ring_r, ring_l, pair_send, pair_recv, z_send, z_recv, x_send, x_recv,
):
    f = lax.axis_index("fsdp")
    t = lax.axis_index("tile")
    nt = nx * nz
    nf_dev = 2 * ny
    y = f // 2
    core = f % 2
    xx = t // nz
    zz = t % nz
    w_hbm = (wq_hbm, wk_hbm, wv_hbm, wo_hbm)
    sh = wq_hbm.shape[0]
    rows, width = tiles_hbm.shape
    hd = width // HEADS
    half = HEADS // 2
    bl = half * hd

    def at_y(d):
        return (((y + d + ny) % ny) * 2 + core, t)

    def at_z(d):
        return (f, xx * nz + (zz + d + nz) % nz)

    def at_x(d):
        return (f, ((xx + d + nx) % nx) * nz + zz)

    def at_t(d):
        return (f, (t + d + nt) % nt)

    pair = (y * 2 + 1 - core, t)

    barrier = pltpu.get_barrier_semaphore()
    peers = [at_t(1), at_t(-1), pair]
    peers += [at_y(d) for d in ((1, -1) if ny > 1 else ())]
    peers += [at_x(d) for d in range(1, nx)]
    peers += [at_z(d) for d in range(1, nz)]
    for p in peers:
        pl.semaphore_signal(barrier, inc=1, device_id=p, device_id_type=MESH)

    load = pltpu.make_async_copy(tiles_hbm, tiles_v, loc_sem.at[0])
    load.start()

    def own_rows(owner_y, owner_core):
        return pl.ds(pl.multiple_of((owner_y * 2 + owner_core) * sh, sh), sh)

    mine = own_rows(y, core)
    own_loads = [pltpu.make_async_copy(w_hbm[w], w_v.at[w, mine, :], loc_sem.at[1 + w]) for w in range(4)]
    for c in own_loads:
        c.start()

    base = t * rows
    own_w = pooling_weights(idx_ref[...], msk_ref[...], base, rows)
    load.wait()
    own_part = exact_dot(own_w, tiles_v[...])
    pl.semaphore_wait(barrier, len(peers))

    def remote(src, dst, send, recv, dev):
        return pltpu.make_async_remote_copy(
            src_ref=src, dst_ref=dst, send_sem=send, recv_sem=recv, device_id=dev, device_id_type=MESH
        )

    def arrived(dst, sem):
        pltpu.make_async_copy(dst, dst, sem).wait()

    halo = []
    for slot, d in ((0, 1), (1, -1)):
        halo.append(remote(idx_ref, nidx.at[slot], halo_send.at[0, slot], halo_recv.at[0, slot], at_t(d)))
        halo.append(remote(msk_ref, nmsk.at[slot], halo_send.at[1, slot], halo_recv.at[1, slot], at_t(d)))
    for c in halo:
        c.start()

    far = ny // 2
    steps_r = [(ny - 1) // 2 + (1 if ny % 2 == 0 and w % 2 == 0 else 0) for w in range(4)]
    steps_l = [(ny - 1) // 2 + (1 if ny % 2 == 0 and w % 2 == 1 else 0) for w in range(4)]
    if ny == 1:
        steps_r = steps_l = [0] * 4

    def slot_of(w, owner_d):
        return w_v.at[w, own_rows((y + owner_d + ny) % ny, core), :]

    def pass_on(w, owner_d):
        ref = w_hbm[w] if owner_d == 0 else slot_of(w, owner_d)
        remote(ref, slot_of(w, owner_d), pair_send.at[w], pair_recv.at[w], pair).start()

    def ring_start(w, s, right):
        d = -(s - 1) if right else s - 1
        ref = w_hbm[w] if s == 1 else slot_of(w, d)
        sem = (ring_r if right else ring_l).at[w, s - 1]
        remote(ref, slot_of(w, d), ring_send.at[w], sem, at_y(1 if right else -1)).start()

    def first(w):
        if steps_r[w] >= 1:
            ring_start(w, 1, True)
        if steps_l[w] >= 1:
            ring_start(w, 1, False)
        pass_on(w, 0)

    def relay(w, s):
        if steps_r[w] >= s:
            arrived(slot_of(w, -s), ring_r.at[w, s - 1])
            if steps_r[w] > s:
                ring_start(w, s + 1, True)
            pass_on(w, -s)
        if steps_l[w] >= s:
            arrived(slot_of(w, s), ring_l.at[w, s - 1])
            if steps_l[w] > s:
                ring_start(w, s + 1, False)
            pass_on(w, s)

    def complete(w):
        own_loads[w].wait()
        whole = w_v.at[w, pl.ds(0, ny * sh), :]
        arrived(whole, pair_recv.at[w])

    def partials():
        for slot, d in ((0, -1), (1, 1)):
            arrived(nidx.at[slot], halo_recv.at[0, slot])
            arrived(nmsk.at[slot], halo_recv.at[1, slot])
            wts = pooling_weights(nidx[slot], nmsk[slot], base, rows)
            pout[slot] = exact_dot(wts, tiles_v[...])
            remote(pout.at[slot], pin.at[1 - slot], halo_send.at[2, slot], halo_recv.at[2, 1 - slot], at_t(d)).start()

    def normed():
        for slot in (0, 1):
            arrived(pin.at[slot], halo_recv.at[2, slot])
        pooled = own_part + pin[0] + pin[1]
        scale = lax.rsqrt(jnp.mean(pooled * pooled, axis=1, keepdims=True) + 1e-06)
        ng[t] = (pooled * scale * gain_ref[...]).astype(BF16)
        for d in range(1, nz):
            e = (d + 1) // 2 if d % 2 else -(d // 2)
            e = e % nz
            remote(ng.at[t], ng.at[t], z_send, z_recv.at[e], at_z(e)).start()
        x_send_block(0)

    def x_send_block(e):
        src = xx * nz + (zz - e + nz) % nz
        for d in range(1, nx):
            remote(ng.at[src], ng.at[src], x_send, x_recv, at_x(d)).start()

    def z_arrival(e):
        src = xx * nz + (zz - e + nz) % nz
        arrived(ng.at[src], z_recv.at[e])
        x_send_block(e)

    def query():
        complete(0)
        q = jnp.dot(tiles_v[...], w_v[0], preferred_element_type=F32)
        qt = q.T.astype(BF16)
        qz[...] = jnp.zeros(qz.shape, BF16)
        for h in range(HEADS):
            g, i = divmod(h, half)
            lo = hd * i - WINDOWS[i][0]
            qz[g, i, lo : lo + hd, :] = qt[h * hd : (h + 1) * hd, :]

    def value_weights():
        complete(2)
        wvt[...] = w_v[2].T

    def gathered():
        if nx > 1:
            many = nz * (nx - 1)
            arrived(ng.at[pl.ds(0, many)], x_recv)
        every = ng[...].astype(F32).reshape(nf.shape[1], width)
        for j in range(nf.shape[0]):
            nf[j] = every[:, j * 128 : (j + 1) * 128]

    def keys_values():
        n_par = nf.shape[1] // 2
        for par in (0, 1):
            n = [nf[j, pl.ds(par, n_par, stride=2), :] for j in range(nf.shape[0])]
            n = jnp.concatenate(n, axis=1).astype(BF16)
            kk[par] = jnp.dot(n, w_v[1], preferred_element_type=F32).astype(BF16)
            vt[par] = lax.dot_general(
                wvt[...], n, (((1,), (1,)), ((), ())), preferred_element_type=F32
            ).astype(BF16)

    def attend():
        n_par = kk.shape[1]
        count = cnt_ref[0]
        factor = math.log2(math.e) / math.sqrt(hd)
        position = lax.broadcasted_iota(jnp.int32, (n_par, rows), 0) * (2 * TILES_PER_KEY)

        @pl.loop(0, 2)
        def _(g):
            for i in range(half):
                par = i % 2
                valid = position + par * TILES_PER_KEY < count
                lo, wide = WINDOWS[i]
                lanes = pl.ds(pl.multiple_of(g * bl + lo, 128), wide)
                score = jnp.dot(kk[par, :, lanes], qz[g, i, :wide, :], preferred_element_type=F32)
                score = jnp.where(valid, score, -jnp.inf)
                top = jnp.max(score, axis=0, keepdims=True)
                weight = jnp.exp2((score - top) * factor)
                total = jnp.sum(weight, axis=0, keepdims=True)
                head = pl.ds(pl.multiple_of(g * bl + i * hd, 16), hd)
                acc = jnp.dot(vt[par, head, :], weight.astype(BF16), preferred_element_type=F32)
                ctxt[head, :] = (acc / total).astype(BF16)

    def project():
        complete(3)
        out_ref[...] = jnp.dot(ctxt[...].T, w_v[3], preferred_element_type=F32).astype(BF16)

    events = []

    def ev(when, fn, *args):
        events.append((when, len(events), fn, args))

    ev(0.1, first, 0)
    ev(0.2, first, 1)
    ev(1.7, partials)
    ev(3.3, relay, 0, 1)
    ev(4.0, normed)
    ev(4.9, relay, 1, 1)
    ev(5.0, first, 2)
    ev(6.5, relay, 0, 2)
    ev(8.0, relay, 1, 2)
    ev(8.1, first, 3)
    ev(9.6, relay, 0, 3)
    ev(11.2, relay, 2, 1)
    ev(12.0, relay, 1, 3)
    ev(12.5, relay, 3, 1)
    ev(13.0, relay, 0, 4)
    ev(13.2, relay, 1, 4)
    ev(13.4, query)
    ev(15.0, relay, 2, 2)
    ev(15.6, relay, 3, 2)
    ev(18.0, relay, 2, 3)
    ev(18.5, relay, 3, 3)
    ev(20.0, relay, 2, 4)
    ev(20.5, relay, 3, 4)
    for d in range(1, nz):
        e = ((d + 1) // 2 if d % 2 else -(d // 2)) % nz
        ev(5.0 + 2.0 + 0.6 * d, z_arrival, e)
    ev(18.1, gathered)
    ev(18.2, complete, 1)
    ev(20.6, value_weights)
    ev(20.7, keys_values)
    ev(20.8, attend)
    ev(21.0, project)
    for _, _, fn, args in sorted(events, key=lambda e: e[:2]):
        fn(*args)

    for c in halo:
        c.wait_send()
    for slot in (0, 1):
        pltpu.make_async_copy(pout.at[slot], pout.at[slot], halo_send.at[2, slot]).wait()
    for w in range(4):
        arrived(w_v.at[w, pl.ds(0, ny * sh), :], pair_send.at[w])
        if ny > 1:
            arrived(w_v.at[w, pl.ds(0, (ny - 1) * sh), :], ring_send.at[w])
    arrived(ng.at[pl.ds(0, nz - 1)], z_send)
    if nx > 1:
        arrived(ng.at[pl.ds(0, nz * (nx - 1))], x_send)


def body(ny, nx, nz, tiles, nbr_tiles, nbr_mask, tile_count, w_query, w_key, w_value, w_out, key_gain):
    rows, width = tiles.shape[1:]
    idx = jnp.transpose(nbr_tiles[0])
    msk = jnp.transpose(nbr_mask[0])
    slots, regions = idx.shape
    keys_dev = regions // REGIONS_PER_KEY
    nt = nx * nz
    keys = keys_dev * nt
    any_space = pl.BlockSpec(memory_space=pl.ANY)
    vmem = pl.BlockSpec(memory_space=pltpu.VMEM)
    dma = pltpu.SemaphoreType.DMA
    out = pl.pallas_call(
        functools.partial(kernel, ny, nx, nz),
        out_shape=jax.ShapeDtypeStruct((rows, width), BF16),
        in_specs=[any_space, vmem, vmem, pl.BlockSpec(memory_space=pltpu.SMEM)] + [any_space] * 4 + [vmem],
        out_specs=vmem,
        scratch_shapes=[
            pltpu.VMEM((rows, width), BF16),
            pltpu.VMEM((4, width, width), BF16),
            pltpu.VMEM((nt, keys_dev, width), BF16),
            pltpu.VMEM((width // 128, keys, 128), F32),
            pltpu.VMEM((2, slots, regions), jnp.int32),
            pltpu.VMEM((2, slots, regions), jnp.int32),
            pltpu.VMEM((2, keys_dev, width), F32),
            pltpu.VMEM((2, keys_dev, width), F32),
            pltpu.VMEM((2, HEADS // 2, 256, rows), BF16),
            pltpu.VMEM((2, keys // 2, width), BF16),
            pltpu.VMEM((2, width, keys // 2), BF16),
            pltpu.VMEM((width, rows), BF16),
            pltpu.VMEM((width, width), BF16),
            dma((5,)),
            dma((3, 2)),
            dma((3, 2)),
            dma((4,)),
            dma((4, 4)),
            dma((4, 4)),
            dma((4,)),
            dma((4,)),
            dma,
            dma((nz,)),
            dma,
            dma,
        ],
        compiler_params=pltpu.CompilerParams(
            collective_id=0, has_side_effects=True, vmem_limit_bytes=56 * 1024 * 1024
        ),
        name="dilated_attention",
    )(tiles[0], idx, msk, tile_count, w_query, w_key, w_value, w_out, key_gain.reshape(1, width))
    return out[None]


def solution(mesh, nz=NZ):
    ny = mesh.shape["fsdp"] // 2
    nx = mesh.shape["tile"] // nz
    placed = (
        P("fsdp", "tile", None),
        P("fsdp", "tile", None),
        P("fsdp", "tile", None),
        P("fsdp"),
        P("fsdp", None),
        P("fsdp", None),
        P("fsdp", None),
        P("fsdp", None),
        P(),
    )
    return jax.shard_map(
        functools.partial(body, ny, nx, nz),
        mesh=mesh, in_specs=placed, out_specs=P("fsdp", "tile", None), check_vma=False,
    )
```

```python
import functools
import math

import jax
import jax.numpy as jnp
from jax import lax
from jax.experimental import pallas as pl
from jax.experimental.pallas import tpu as pltpu
from jax.sharding import PartitionSpec as P

HEADS = 16
REGIONS_PER_KEY = 8
TILES_PER_KEY = 32
NZ = 16
MESH = pl.DeviceIdType.MESH
BF16 = jnp.bfloat16
GROUPS = ((0,), (1, 2, 3), (4, 5, 6, 7), (8, 9, 10, 11), (12, 13, 14), (15,))
F32 = jnp.float32
WINDOWS = ((0, 128), (0, 128), (0, 256), (128, 128), (128, 128), (128, 256), (256, 128), (256, 128))


def pooling_weights(idx, msk, base, rows):
    m = msk.astype(F32)
    share = m / jnp.maximum(jnp.sum(m, axis=0, keepdims=True), 1.0)
    at = idx - base
    slots, regions = idx.shape
    tile = lax.broadcasted_iota(jnp.int32, (rows, regions), 0)
    acc = jnp.zeros((rows, regions), F32)
    for s in range(slots):
        acc = acc + jnp.where(tile == at[s : s + 1, :], share[s : s + 1, :], 0.0)
    acc = acc.T
    keys = regions // REGIONS_PER_KEY
    return jnp.sum(acc.reshape(keys, REGIONS_PER_KEY, rows), axis=1) * (1.0 / REGIONS_PER_KEY)


def exact_dot(w, x):
    hi = w.astype(BF16)
    rest = w - hi.astype(F32)
    mid = rest.astype(BF16)
    low = (rest - mid.astype(F32)).astype(BF16)
    n = w.shape[0]
    parts = jnp.concatenate([hi.astype(F32), mid.astype(F32), low.astype(F32)], axis=0).astype(BF16)
    y = jnp.dot(parts, x, preferred_element_type=F32)
    return y[:n] + y[n : 2 * n] + y[2 * n :]


STARTS = (0.0, 2.6, 5.0, 5.2, 7.3, 8.8, 10.3, 10.0, 12.7, 12.7, 14.8, 15.7, 15.2, 16.2, 18.0, 15.9)
RELAYS = ((0, 1), (1, 1), (0, 2), (1, 2), (0, 3), (1, 3), (0, 4), (1, 4))


def chunks(nz):
    if nz == len(STARTS):
        return ((0, 1), (1, 5), (5, 9), (9, 13), (13, 16))
    return ((0, 1), (1, nz))


def expected(nz):
    start = [STARTS[z * (len(STARTS) - 1) // max(nz - 1, 1)] for z in range(nz)]

    def dist(a, b):
        d = abs(a - b)
        return min(d, nz - d)

    def data(d):
        return 0.9 + 0.77 * d

    def signal(d):
        return 0.25 + 0.7 * d

    ready = [max(start[max(z - 1, 0) : z + 2]) + 2.0 for z in range(nz)]
    up = ready
    last = nz - 1
    arrive = {}
    for z in range(nz):
        if z > 0:
            arrive[z, 0] = max(ready[z], ready[z - 1] + data(1))
        if z < last:
            arrive[z, 1] = max(ready[z], ready[z + 1] + data(1))
    arrive[0, 0] = up[last] + data(2)
    arrive[last, 1] = arrive[0, 0] + data(2)
    part = {k: v + 0.6 for k, v in arrive.items()}
    norm = []
    for z in range(nz):
        left = part[z - 1, 1] + data(1) if z > 0 else part[last, 1] + data(2)
        right = part[z + 1, 0] + data(1) if z < last else part[0, 0] + data(2)
        norm.append(max(left, right, up[z], part[z, 0], part[z, 1]) + 0.3)
    sent = {}
    for z in range(nz):
        for e in range(1, nz):
            to = z + e
            sent[z, e] = norm[z] if to >= nz else max(norm[z], up[to] + signal(dist(z, to)))
    plans = []
    for z in range(nz):
        p = [(arrive[z, 0], "part", 0), (arrive[z, 1], "part", 1), (norm[z], "norm", None)]
        for i, ws in enumerate(RELAYS):
            p.append((ready[z] + 1.7 + 3.4 * (i + 1 if i < 6 else 7), "relay", ws))
        for e in range(1, nz):
            if z + e < nz:
                p.append((sent[z, e], "zsend", z + e))
            src = (z - e) % nz
            p.append((sent[src, e] + data(dist(z, src)) + 0.3, "zarr", src))
        got = {src: tm for tm, kind, src in p if kind == "zarr"}
        got[z] = norm[z]
        for lo, hi in chunks(nz):
            p.append((max(got[src] for src in range(lo, hi)), "xsend", (lo, hi)))
        plans.append(p)
    return plans


def orders(nz):
    plans = expected(nz)
    groups = GROUPS if nz == len(STARTS) else tuple((z,) for z in range(nz))
    out = []
    for members in groups:
        when = {}
        for z in members:
            for tm, kind, arg in plans[z]:
                when[kind, arg] = max(tm, when.get((kind, arg), 0.0))
        done = when["norm", None]
        when = {k: max(tm, done + 0.01) if k[0] in ("zsend", "xsend") else tm for k, tm in when.items()}
        cuts = [-1.0] + [max(when["relay", (b, s)] for s in range(1, 5)) + 0.9 + b for b in (0, 1)] + [1e9]
        listed = sorted(when.items(), key=lambda it: it[1])
        stages = [[k for k, tm in listed if lo < tm <= hi] for lo, hi in zip(cuts[:-1], cuts[1:])]
        out.append((members, stages))
    return out


def kernel(
    ny, nx, nz,
    tiles_hbm, idx_hbm, msk_hbm, cnt_ref, wq_hbm, wk_hbm, wv_hbm, wo_hbm, gain_hbm,
    out_ref,
    tiles_v, w_v, ng, nf, oidx, omsk, ogain, nidx, nmsk, pown, pout, pin, qz, kk, vt, ctxt, wvt,
    loc_sem, halo_send, halo_recv, ring_send, ring_r, ring_l, pair_send, pair_recv, z_send, z_recv, x_send, x_recv,
    here_sem,
):
    f = lax.axis_index("fsdp")
    t = lax.axis_index("tile")
    nt = nx * nz
    y = f // 2
    core = f % 2
    xx = t // nz
    zz = t % nz
    w_hbm = (wq_hbm, wk_hbm, wv_hbm, wo_hbm)
    sh = wq_hbm.shape[0]
    rows, width = tiles_hbm.shape
    hd = width // HEADS
    half = HEADS // 2
    bl = half * hd

    def at_y(d):
        return (((y + d + ny) % ny) * 2 + core, t)

    def at_z(d):
        return (f, xx * nz + (zz + d + nz) % nz)

    def at_x(d):
        return (f, ((xx + d + nx) % nx) * nz + zz)

    def at_t(d):
        return (f, (t + d + nt) % nt)

    pair = (y * 2 + 1 - core, t)

    barrier = pltpu.get_barrier_semaphore()

    def greet(dev, sem=barrier):
        pl.semaphore_signal(sem, inc=1, device_id=dev, device_id_type=MESH)

    near = [pair]
    near += [at_y(d) for d in ((1, -1) if ny > 1 else ())]
    near += [at_x(d) for d in range(1, nx)]
    for p in near:
        greet(p)
    is_first = zz == 0
    is_last = zz == nz - 1

    @pl.when(jnp.logical_not(is_first))
    def _():
        greet(at_z(-1))

    @pl.when(is_first)
    def _():
        greet(at_t(-1))

    for k in range(1, nz):
        @pl.when(zz + k < nz)
        def _(k=k):
            greet(at_z(k))

    loads = [
        pltpu.make_async_copy(src, dst, loc_sem.at[i])
        for i, (src, dst) in enumerate(
            [(tiles_hbm, tiles_v), (idx_hbm, oidx), (msk_hbm, omsk), (gain_hbm, ogain)]
            + [(w_hbm[w], w_v.at[f, w]) for w in range(4)]
        )
    ]
    for c in loads:
        c.start()
    own_loads = loads[4:]
    pl.semaphore_wait(barrier, len(near) + zz + 1)

    def remote(src, dst, send, recv, dev):
        return pltpu.make_async_remote_copy(
            src_ref=src, dst_ref=dst, send_sem=send, recv_sem=recv, device_id=dev, device_id_type=MESH
        )

    def arrived(dst, sem):
        pltpu.make_async_copy(dst, dst, sem).wait()

    def lists_to(d):
        slot = 0 if d == 1 else 1
        remote(idx_hbm, nidx.at[slot], halo_send.at[0, slot], halo_recv.at[0, slot], at_t(d)).start()
        remote(msk_hbm, nmsk.at[slot], halo_send.at[1, slot], halo_recv.at[1, slot], at_t(d)).start()

    steps_r = [(ny - 1) // 2 + (1 if ny % 2 == 0 and b % 2 == 0 else 0) for b in range(2)]
    steps_l = [(ny - 1) // 2 + (1 if ny % 2 == 0 and b % 2 == 1 else 0) for b in range(2)]

    def slot_of(b, owner_d):
        return w_v.at[((y + owner_d + ny) % ny) * 2 + core, pl.ds(2 * b, 2)]

    def pass_on(b, owner_d):
        ref = slot_of(b, owner_d)
        remote(ref, ref, pair_send.at[b], pair_recv.at[b], pair).start()

    def ring_start(b, s, right):
        ref = slot_of(b, -(s - 1) if right else s - 1)
        sem = (ring_r if right else ring_l).at[b, s - 1]
        remote(ref, ref, ring_send.at[b], sem, at_y(1 if right else -1)).start()

    def relay(b, s):
        if steps_r[b] >= s:
            arrived(slot_of(b, -s), ring_r.at[b, s - 1])
            if steps_r[b] > s:
                ring_start(b, s + 1, True)
            pass_on(b, -s)
        if steps_l[b] >= s:
            arrived(slot_of(b, s), ring_l.at[b, s - 1])
            if steps_l[b] > s:
                ring_start(b, s + 1, False)
            pass_on(b, s)

    def complete(b):
        arrived(w_v.at[pl.ds(0, ny), pl.ds(2 * b, 2)], pair_recv.at[b])

    def weight(w):
        return w_v[:, w].reshape(width, width)

    lists_to(1)

    @pl.when(jnp.logical_not(is_first))
    def _():
        lists_to(-1)

    for k in range(1, nz):
        @pl.when(k <= zz)
        def _(k=k):
            greet(at_z(-k), here_sem.at[zz])

    for b in range(2):
        for c in own_loads[2 * b : 2 * b + 2]:
            c.wait()
        if steps_r[b] >= 1:
            ring_start(b, 1, True)
        if steps_l[b] >= 1:
            ring_start(b, 1, False)
    for b in range(2):
        pass_on(b, 0)

    base = t * rows
    for c in loads[:4]:
        c.wait()
    pown[...] = exact_dot(pooling_weights(oidx[...], omsk[...], base, rows), tiles_v[...])

    def part(slot):
        d = -1 if slot == 0 else 1
        arrived(nidx.at[slot], halo_recv.at[0, slot])
        arrived(nmsk.at[slot], halo_recv.at[1, slot])
        if slot == 0:
            @pl.when(is_first)
            def _():
                lists_to(-1)

        wts = pooling_weights(nidx[slot], nmsk[slot], base, rows)
        pout[slot] = exact_dot(wts, tiles_v[...])
        remote(pout.at[slot], pin.at[1 - slot], halo_send.at[2, slot], halo_recv.at[2, 1 - slot], at_t(d)).start()

    def norm():
        for slot in (0, 1):
            arrived(pin.at[slot], halo_recv.at[2, slot])
        pooled = pown[...] + pin[0] + pin[1]
        scale = lax.rsqrt(jnp.mean(pooled * pooled, axis=1, keepdims=True) + 1e-06)
        ng[t] = (pooled * scale * ogain[...].reshape(1, width)).astype(BF16)
        for d in range(1, nz):
            e = ((d + 1) // 2 if d % 2 else -(d // 2)) % nz

            @pl.when(zz + e >= nz)
            def _(e=e):
                z_block(zz + e - nz)


    def z_block(to):
        remote(ng.at[t], ng.at[t], z_send, z_recv.at[zz], (f, xx * nz + to)).start()

    def zsend(to):
        @pl.when(to > zz)
        def _():
            pl.semaphore_wait(here_sem.at[to], 1)
            z_block(to)

    def xsend(span):
        lo, hi = span
        block = ng.at[pl.ds(xx * nz + lo, hi - lo)]
        for d in range(1, nx):
            remote(block, block, x_send, x_recv, at_x(d)).start()

    def zarr(src):
        @pl.when(src != zz)
        def _():
            arrived(ng.at[xx * nz + src], z_recv.at[src])

    handlers = {
        "part": part, "norm": lambda _: norm(), "relay": lambda ws: relay(*ws),
        "zsend": zsend, "zarr": zarr, "xsend": xsend,
    }
    listed = orders(nz)

    def run(stage):
        for members, stages in listed:
            @pl.when(jnp.logical_and(zz >= members[0], zz <= members[-1]))
            def _(todo=stages[stage]):
                for kind, arg in todo:
                    handlers[kind](arg)

    def query():
        complete(0)
        q = jnp.dot(tiles_v[...], weight(0), preferred_element_type=F32)
        qt = q.T.astype(BF16)
        qz[...] = jnp.zeros(qz.shape, BF16)
        for h in range(HEADS):
            g, i = divmod(h, half)
            lo = hd * i - WINDOWS[i][0]
            qz[g, i, lo : lo + hd, :] = qt[h * hd : (h + 1) * hd, :]

    def value_weights():
        complete(1)
        wvt[...] = weight(2).T

    def gathered():
        if nx > 1:
            many = nz * (nx - 1)
            arrived(ng.at[pl.ds(0, many)], x_recv)
        every = ng[...].astype(F32).reshape(nf.shape[1], width)
        for j in range(nf.shape[0]):
            nf[j] = every[:, j * 128 : (j + 1) * 128]

    def keys_values():
        n_par = nf.shape[1] // 2
        for par in (0, 1):
            n = [nf[j, pl.ds(par, n_par, stride=2), :] for j in range(nf.shape[0])]
            n = jnp.concatenate(n, axis=1).astype(BF16)
            kk[par] = jnp.dot(n, weight(1), preferred_element_type=F32).astype(BF16)
            vt[par] = lax.dot_general(
                wvt[...], n, (((1,), (1,)), ((), ())), preferred_element_type=F32
            ).astype(BF16)

    def attend():
        n_par = kk.shape[1]
        count = cnt_ref[0]
        factor = math.log2(math.e) / math.sqrt(hd)
        position = lax.broadcasted_iota(jnp.int32, (n_par, rows), 0) * (2 * TILES_PER_KEY)

        @pl.loop(0, 2)
        def _(g):
            for i in range(half):
                par = i % 2
                valid = position + par * TILES_PER_KEY < count
                lo, wide = WINDOWS[i]
                lanes = pl.ds(pl.multiple_of(g * bl + lo, 128), wide)
                score = jnp.dot(kk[par, :, lanes], qz[g, i, :wide, :], preferred_element_type=F32)
                score = jnp.where(valid, score, -jnp.inf)
                top = jnp.max(score, axis=0, keepdims=True)
                weight = jnp.exp2((score - top) * factor)
                total = jnp.sum(weight, axis=0, keepdims=True)
                head = pl.ds(pl.multiple_of(g * bl + i * hd, 16), hd)
                acc = jnp.dot(vt[par, head, :], weight.astype(BF16), preferred_element_type=F32)
                ctxt[head, :] = (acc / total).astype(BF16)

    def project():
        out_ref[...] = jnp.dot(ctxt[...].T, weight(3), preferred_element_type=F32).astype(BF16)

    run(0)
    query()
    run(1)
    value_weights()
    run(2)
    gathered()
    keys_values()
    attend()
    project()

    for slot in (0, 1):
        arrived(nidx.at[slot], halo_send.at[0, slot])
        arrived(nmsk.at[slot], halo_send.at[1, slot])
        arrived(pout.at[slot], halo_send.at[2, slot])
    for b in range(2):
        arrived(w_v.at[pl.ds(0, ny), pl.ds(2 * b, 2)], pair_send.at[b])
        if ny > 1:
            arrived(w_v.at[pl.ds(0, ny - 1), pl.ds(2 * b, 2)], ring_send.at[b])
    arrived(ng.at[pl.ds(0, nz - 1)], z_send)
    if nx > 1:
        arrived(ng.at[pl.ds(0, nz * (nx - 1))], x_send)


def body(ny, nx, nz, tiles, nbr_tiles, nbr_mask, tile_count, w_query, w_key, w_value, w_out, key_gain):
    rows, width = tiles.shape[1:]
    idx = jnp.transpose(nbr_tiles[0])
    msk = jnp.transpose(nbr_mask[0])
    slots, regions = idx.shape
    keys_dev = regions // REGIONS_PER_KEY
    nt = nx * nz
    keys = keys_dev * nt
    any_space = pl.BlockSpec(memory_space=pl.ANY)
    vmem = pl.BlockSpec(memory_space=pltpu.VMEM)
    dma = pltpu.SemaphoreType.DMA
    out = pl.pallas_call(
        functools.partial(kernel, ny, nx, nz),
        out_shape=jax.ShapeDtypeStruct((rows, width), BF16),
        in_specs=[any_space] * 3 + [pl.BlockSpec(memory_space=pltpu.SMEM)] + [any_space] * 5,
        out_specs=vmem,
        scratch_shapes=[
            pltpu.VMEM((rows, width), BF16),
            pltpu.VMEM((2 * ny, 4, width // (2 * ny), width), BF16),
            pltpu.VMEM((nt, keys_dev, width), BF16),
            pltpu.VMEM((width // 128, keys, 128), F32),
            pltpu.VMEM((slots, regions), jnp.int32),
            pltpu.VMEM((slots, regions), jnp.int32),
            pltpu.VMEM((width,), F32),
            pltpu.VMEM((2, slots, regions), jnp.int32),
            pltpu.VMEM((2, slots, regions), jnp.int32),
            pltpu.VMEM((keys_dev, width), F32),
            pltpu.VMEM((2, keys_dev, width), F32),
            pltpu.VMEM((2, keys_dev, width), F32),
            pltpu.VMEM((2, HEADS // 2, 256, rows), BF16),
            pltpu.VMEM((2, keys // 2, width), BF16),
            pltpu.VMEM((2, width, keys // 2), BF16),
            pltpu.VMEM((width, rows), BF16),
            pltpu.VMEM((width, width), BF16),
            dma((8,)),
            dma((3, 2)),
            dma((3, 2)),
            dma((2,)),
            dma((2, 4)),
            dma((2, 4)),
            dma((2,)),
            dma((2,)),
            dma,
            dma((nz,)),
            dma,
            dma,
            pltpu.SemaphoreType.REGULAR((nz,)),
        ],
        compiler_params=pltpu.CompilerParams(
            collective_id=0, has_side_effects=True, vmem_limit_bytes=56 * 1024 * 1024
        ),
        name="dilated_attention",
    )(tiles[0], idx, msk, tile_count, w_query, w_key, w_value, w_out, key_gain)
    return out[None]


def solution(mesh, nz=NZ):
    ny = mesh.shape["fsdp"] // 2
    nx = mesh.shape["tile"] // nz
    placed = (
        P("fsdp", "tile", None),
        P("fsdp", "tile", None),
        P("fsdp", "tile", None),
        P("fsdp"),
        P("fsdp", None),
        P("fsdp", None),
        P("fsdp", None),
        P("fsdp", None),
        P(),
    )
    return jax.shard_map(
        functools.partial(body, ny, nx, nz),
        mesh=mesh, in_specs=placed, out_specs=P("fsdp", "tile", None), check_vma=False,
    )
```

```python
import functools
import math

import jax
import jax.numpy as jnp
from jax import lax
from jax.experimental import pallas as pl
from jax.experimental.pallas import tpu as pltpu
from jax.sharding import PartitionSpec as P

HEADS = 16
REGIONS_PER_KEY = 8
TILES_PER_KEY = 32
NZ = 16
MESH = pl.DeviceIdType.MESH
BF16 = jnp.bfloat16
GROUPS = ((0,), (1, 2, 3), (4, 5, 6, 7), (8, 9, 10, 11), (12, 13, 14), (15,))
F32 = jnp.float32
WINDOWS = ((0, 128), (0, 128), (0, 256), (128, 128), (128, 128), (128, 256), (256, 128), (256, 128))


def pooling_weights(idx, msk, base, rows):
    m = msk.astype(F32)
    share = m / jnp.maximum(jnp.sum(m, axis=0, keepdims=True), 1.0)
    at = idx - base
    slots, regions = idx.shape
    tile = lax.broadcasted_iota(jnp.int32, (rows, regions), 0)
    acc = jnp.zeros((rows, regions), F32)
    for s in range(slots):
        acc = acc + jnp.where(tile == at[s : s + 1, :], share[s : s + 1, :], 0.0)
    acc = acc.T
    keys = regions // REGIONS_PER_KEY
    return jnp.sum(acc.reshape(keys, REGIONS_PER_KEY, rows), axis=1) * (1.0 / REGIONS_PER_KEY)


def exact_dot(w, x):
    hi = w.astype(BF16)
    rest = w - hi.astype(F32)
    mid = rest.astype(BF16)
    low = (rest - mid.astype(F32)).astype(BF16)
    n = w.shape[0]
    parts = jnp.concatenate([hi.astype(F32), mid.astype(F32), low.astype(F32)], axis=0).astype(BF16)
    y = jnp.dot(parts, x, preferred_element_type=F32)
    return y[:n] + y[n : 2 * n] + y[2 * n :]


STARTS = (0.0, 2.6, 5.0, 5.2, 7.3, 8.8, 10.3, 10.0, 12.7, 12.7, 14.8, 15.7, 15.2, 16.2, 18.0, 15.9)
LATE_RING = 13.0
SLACK = 4.0
RELAYS = ((0, 1), (1, 1), (0, 2), (1, 2), (0, 3), (1, 3), (0, 4), (1, 4))


def chunks(nz):
    if nz == len(STARTS):
        return ((0, 1), (1, 5), (5, 9), (9, 13), (13, 16))
    return ((0, 1), (1, nz))


def expected(nz, ring_from=0.0):
    start = [STARTS[z * (len(STARTS) - 1) // max(nz - 1, 1)] for z in range(nz)]

    def dist(a, b):
        d = abs(a - b)
        return min(d, nz - d)

    def data(d):
        return 0.9 + 0.77 * d

    def signal(d):
        return 0.25 + 0.7 * d

    ready = [max(start[max(z - 1, 0) : z + 2]) + 2.0 for z in range(nz)]
    up = ready
    last = nz - 1
    arrive = {}
    for z in range(nz):
        if z > 0:
            arrive[z, 0] = max(ready[z], ready[z - 1] + data(1))
        if z < last:
            arrive[z, 1] = max(ready[z], ready[z + 1] + data(1))
    arrive[0, 0] = up[last] + data(2)
    arrive[last, 1] = arrive[0, 0] + data(2)
    part = {k: v + 0.6 for k, v in arrive.items()}
    norm = []
    for z in range(nz):
        left = part[z - 1, 1] + data(1) if z > 0 else part[last, 1] + data(2)
        right = part[z + 1, 0] + data(1) if z < last else part[0, 0] + data(2)
        norm.append(max(left, right, up[z], part[z, 0], part[z, 1]) + 0.3)
    sent = {}
    for z in range(nz):
        for e in range(1, nz):
            to = z + e
            sent[z, e] = norm[z] if to >= nz else max(norm[z], up[to] + signal(dist(z, to)))
    plans = []
    for z in range(nz):
        p = [(arrive[z, 0], "part", 0), (arrive[z, 1], "part", 1), (norm[z], "norm", None)]
        for i, ws in enumerate(RELAYS):
            pace = 2.2 if ring_from else 3.4
            tm = max(ready[z], ring_from) + 1.7 + pace * (i + 1 if i < 6 else 7)
            close = 1.5 if ring_from else 3.0
            p.append((norm[z] + 1.1 + 0.01 * i if norm[z] - close < tm < norm[z] + 1.0 else tm, "relay", ws))
        for e in range(1, nz):
            if z + e < nz:
                p.append((sent[z, e] + 1.0, "zsend", z + e))
            src = (z - e) % nz
            p.append((sent[src, e] + data(dist(z, src)) + SLACK, "zarr", src))
        got = {src: tm for tm, kind, src in p if kind == "zarr"}
        got[z] = norm[z]
        for lo, hi in chunks(nz):
            p.append((max(got[src] for src in range(lo, hi)), "xsend", (lo, hi)))
        plans.append(p)
    return plans


def orders(nz):
    out = []
    for members in GROUPS if nz == len(STARTS) else tuple((z,) for z in range(nz)):
        if STARTS[members[0]] < LATE_RING:
            out.append((members, (0,), order_of(members, expected(nz, LATE_RING))))
            out.append((members, (1, 2, 3), order_of(members, expected(nz))))
        else:
            out.append((members, (0, 1, 2, 3), order_of(members, expected(nz))))
    return out


def order_of(members, plans):
    when = {}
    for z in members:
        for tm, kind, arg in plans[z]:
            when[kind, arg] = max(tm, when.get((kind, arg), 0.0))
    done = when["norm", None]
    when = {k: max(tm, done + 0.01) if k[0] in ("zsend", "xsend") else tm for k, tm in when.items()}
    cuts = [-1.0] + [max(when["relay", (b, s)] for s in range(1, 5)) + 0.9 + b for b in (0, 1)] + [1e9]
    listed = sorted(when.items(), key=lambda it: it[1])
    return [[k for k, tm in listed if lo < tm <= hi] for lo, hi in zip(cuts[:-1], cuts[1:])]


def kernel(
    ny, nx, nz,
    tiles_hbm, idx_hbm, msk_hbm, cnt_ref, wq_hbm, wk_hbm, wv_hbm, wo_hbm, gain_hbm,
    out_ref,
    tiles_v, w_v, ng, nf, oidx, omsk, ogain, nidx, nmsk, pown, pout, pin, qz, kk, vt, ctxt, wvt,
    loc_sem, halo_send, halo_recv, ring_send, ring_r, ring_l, pair_send, pair_recv, z_send, z_recv, x_send, x_recv,
    here_sem,
):
    f = lax.axis_index("fsdp")
    t = lax.axis_index("tile")
    nt = nx * nz
    y = f // 2
    core = f % 2
    xx = t // nz
    zz = t % nz
    w_hbm = (wq_hbm, wk_hbm, wv_hbm, wo_hbm)
    sh = wq_hbm.shape[0]
    rows, width = tiles_hbm.shape
    hd = width // HEADS
    half = HEADS // 2
    bl = half * hd

    def at_y(d):
        return (((y + d + ny) % ny) * 2 + core, t)

    def at_z(d):
        return (f, xx * nz + (zz + d + nz) % nz)

    def at_x(d):
        return (f, ((xx + d + nx) % nx) * nz + zz)

    def at_t(d):
        return (f, (t + d + nt) % nt)

    pair = (y * 2 + 1 - core, t)

    barrier = pltpu.get_barrier_semaphore()

    def greet(dev, sem=barrier):
        pl.semaphore_signal(sem, inc=1, device_id=dev, device_id_type=MESH)

    near = [pair]
    near += [at_y(d) for d in ((1, -1) if ny > 1 else ())]
    near += [at_x(d) for d in range(1, nx)]
    for p in near:
        greet(p)
    is_first = zz == 0
    is_last = zz == nz - 1

    @pl.when(jnp.logical_not(is_first))
    def _():
        greet(at_z(-1))

    @pl.when(is_first)
    def _():
        greet(at_t(-1))

    for k in range(1, nz):
        @pl.when(zz + k < nz)
        def _(k=k):
            greet(at_z(k))

    loads = [
        pltpu.make_async_copy(src, dst, loc_sem.at[i])
        for i, (src, dst) in enumerate(
            [(tiles_hbm, tiles_v), (idx_hbm, oidx), (msk_hbm, omsk), (gain_hbm, ogain)]
            + [(w_hbm[w], w_v.at[f, w]) for w in range(4)]
        )
    ]
    for c in loads:
        c.start()
    own_loads = loads[4:]
    pl.semaphore_wait(barrier, len(near) + zz + 1)

    def remote(src, dst, send, recv, dev):
        return pltpu.make_async_remote_copy(
            src_ref=src, dst_ref=dst, send_sem=send, recv_sem=recv, device_id=dev, device_id_type=MESH
        )

    def arrived(dst, sem):
        pltpu.make_async_copy(dst, dst, sem).wait()

    def lists_to(d):
        slot = 0 if d == 1 else 1
        remote(idx_hbm, nidx.at[slot], halo_send.at[0, slot], halo_recv.at[0, slot], at_t(d)).start()
        remote(msk_hbm, nmsk.at[slot], halo_send.at[1, slot], halo_recv.at[1, slot], at_t(d)).start()

    steps_r = [(ny - 1) // 2 + (1 if ny % 2 == 0 and b % 2 == 0 else 0) for b in range(2)]
    steps_l = [(ny - 1) // 2 + (1 if ny % 2 == 0 and b % 2 == 1 else 0) for b in range(2)]

    def slot_of(b, owner_d):
        return w_v.at[((y + owner_d + ny) % ny) * 2 + core, pl.ds(2 * b, 2)]

    def pass_on(b, owner_d):
        ref = slot_of(b, owner_d)
        remote(ref, ref, pair_send.at[b], pair_recv.at[b], pair).start()

    def ring_start(b, s, right):
        ref = slot_of(b, -(s - 1) if right else s - 1)
        sem = (ring_r if right else ring_l).at[b, s - 1]
        remote(ref, ref, ring_send.at[b], sem, at_y(1 if right else -1)).start()

    def relay(b, s):
        if steps_r[b] >= s:
            arrived(slot_of(b, -s), ring_r.at[b, s - 1])
            if steps_r[b] > s:
                ring_start(b, s + 1, True)
            pass_on(b, -s)
        if steps_l[b] >= s:
            arrived(slot_of(b, s), ring_l.at[b, s - 1])
            if steps_l[b] > s:
                ring_start(b, s + 1, False)
            pass_on(b, s)

    def complete(b):
        arrived(w_v.at[pl.ds(0, ny), pl.ds(2 * b, 2)], pair_recv.at[b])

    def weight(w):
        return w_v[:, w].reshape(width, width)

    lists_to(1)

    @pl.when(jnp.logical_not(is_first))
    def _():
        lists_to(-1)

    for k in range(1, nz):
        @pl.when(k <= zz)
        def _(k=k):
            greet(at_z(-k), here_sem.at[zz])

    for b in range(2):
        for c in own_loads[2 * b : 2 * b + 2]:
            c.wait()
        if steps_r[b] >= 1:
            ring_start(b, 1, True)
        if steps_l[b] >= 1:
            ring_start(b, 1, False)
    for b in range(2):
        pass_on(b, 0)

    base = t * rows
    for c in loads[:4]:
        c.wait()
    pown[...] = exact_dot(pooling_weights(oidx[...], omsk[...], base, rows), tiles_v[...])

    def part(slot):
        d = -1 if slot == 0 else 1
        arrived(nidx.at[slot], halo_recv.at[0, slot])
        arrived(nmsk.at[slot], halo_recv.at[1, slot])
        if slot == 0:
            @pl.when(is_first)
            def _():
                lists_to(-1)

        wts = pooling_weights(nidx[slot], nmsk[slot], base, rows)
        pout[slot] = exact_dot(wts, tiles_v[...])
        remote(pout.at[slot], pin.at[1 - slot], halo_send.at[2, slot], halo_recv.at[2, 1 - slot], at_t(d)).start()

    def norm():
        for slot in (0, 1):
            arrived(pin.at[slot], halo_recv.at[2, slot])
        pooled = pown[...] + pin[0] + pin[1]
        scale = lax.rsqrt(jnp.mean(pooled * pooled, axis=1, keepdims=True) + 1e-06)
        ng[t] = (pooled * scale * ogain[...].reshape(1, width)).astype(BF16)
        for d in range(1, nz):
            e = ((d + 1) // 2 if d % 2 else -(d // 2)) % nz

            @pl.when(zz + e >= nz)
            def _(e=e):
                z_block(zz + e - nz)


    def z_block(to):
        remote(ng.at[t], ng.at[t], z_send, z_recv.at[zz], (f, xx * nz + to)).start()

    def zsend(to):
        @pl.when(to > zz)
        def _():
            pl.semaphore_wait(here_sem.at[to], 1)
            z_block(to)

    def xsend(span):
        lo, hi = span
        block = ng.at[pl.ds(xx * nz + lo, hi - lo)]
        for d in range(1, nx):
            remote(block, block, x_send, x_recv, at_x(d)).start()

    def zarr(src):
        @pl.when(src != zz)
        def _():
            arrived(ng.at[xx * nz + src], z_recv.at[src])

    handlers = {
        "part": part, "norm": lambda _: norm(), "relay": lambda ws: relay(*ws),
        "zsend": zsend, "zarr": zarr, "xsend": xsend,
    }
    listed = orders(nz)

    def run(stage):
        for members, columns, stages in listed:
            rows_in = jnp.logical_and(zz >= members[0], zz <= members[-1])

            @pl.when(jnp.logical_and(rows_in, jnp.logical_and(xx >= columns[0], xx <= columns[-1])))
            def _(todo=stages[stage]):
                for kind, arg in todo:
                    handlers[kind](arg)

    def query():
        complete(0)
        q = jnp.dot(tiles_v[...], weight(0), preferred_element_type=F32)
        qt = q.T.astype(BF16)
        qz[...] = jnp.zeros(qz.shape, BF16)
        for h in range(HEADS):
            g, i = divmod(h, half)
            lo = hd * i - WINDOWS[i][0]
            qz[g, i, lo : lo + hd, :] = qt[h * hd : (h + 1) * hd, :]

    def value_weights():
        complete(1)
        wvt[...] = weight(2).T

    def gathered():
        if nx > 1:
            many = nz * (nx - 1)
            arrived(ng.at[pl.ds(0, many)], x_recv)
        every = ng[...].astype(F32).reshape(nf.shape[1], width)
        for j in range(nf.shape[0]):
            nf[j] = every[:, j * 128 : (j + 1) * 128]

    def keys_values():
        n_par = nf.shape[1] // 2
        for par in (0, 1):
            n = [nf[j, pl.ds(par, n_par, stride=2), :] for j in range(nf.shape[0])]
            n = jnp.concatenate(n, axis=1).astype(BF16)
            kk[par] = jnp.dot(n, weight(1), preferred_element_type=F32).astype(BF16)
            vt[par] = lax.dot_general(
                wvt[...], n, (((1,), (1,)), ((), ())), preferred_element_type=F32
            ).astype(BF16)

    def attend():
        n_par = kk.shape[1]
        count = cnt_ref[0]
        factor = math.log2(math.e) / math.sqrt(hd)
        position = lax.broadcasted_iota(jnp.int32, (n_par, rows), 0) * (2 * TILES_PER_KEY)

        @pl.loop(0, 2)
        def _(g):
            for i in range(half):
                par = i % 2
                valid = position + par * TILES_PER_KEY < count
                lo, wide = WINDOWS[i]
                lanes = pl.ds(pl.multiple_of(g * bl + lo, 128), wide)
                score = jnp.dot(kk[par, :, lanes], qz[g, i, :wide, :], preferred_element_type=F32)
                score = jnp.where(valid, score, -jnp.inf)
                top = jnp.max(score, axis=0, keepdims=True)
                weight = jnp.exp2((score - top) * factor)
                total = jnp.sum(weight, axis=0, keepdims=True)
                head = pl.ds(pl.multiple_of(g * bl + i * hd, 16), hd)
                acc = jnp.dot(vt[par, head, :], weight.astype(BF16), preferred_element_type=F32)
                ctxt[head, :] = (acc / total).astype(BF16)

    def project():
        out_ref[...] = jnp.dot(ctxt[...].T, weight(3), preferred_element_type=F32).astype(BF16)

    run(0)
    query()
    run(1)
    value_weights()
    run(2)
    gathered()
    keys_values()
    attend()
    project()

    for slot in (0, 1):
        arrived(nidx.at[slot], halo_send.at[0, slot])
        arrived(nmsk.at[slot], halo_send.at[1, slot])
        arrived(pout.at[slot], halo_send.at[2, slot])
    for b in range(2):
        arrived(w_v.at[pl.ds(0, ny), pl.ds(2 * b, 2)], pair_send.at[b])
        if ny > 1:
            arrived(w_v.at[pl.ds(0, ny - 1), pl.ds(2 * b, 2)], ring_send.at[b])
    arrived(ng.at[pl.ds(0, nz - 1)], z_send)
    if nx > 1:
        arrived(ng.at[pl.ds(0, nz * (nx - 1))], x_send)


def body(ny, nx, nz, tiles, nbr_tiles, nbr_mask, tile_count, w_query, w_key, w_value, w_out, key_gain):
    rows, width = tiles.shape[1:]
    idx = jnp.transpose(nbr_tiles[0])
    msk = jnp.transpose(nbr_mask[0])
    slots, regions = idx.shape
    keys_dev = regions // REGIONS_PER_KEY
    nt = nx * nz
    keys = keys_dev * nt
    keep = functools.partial(pltpu.with_memory_space_constraint, memory_space=pltpu.HBM)
    any_space = pl.BlockSpec(memory_space=pl.ANY)
    vmem = pl.BlockSpec(memory_space=pltpu.VMEM)
    dma = pltpu.SemaphoreType.DMA
    out = pl.pallas_call(
        functools.partial(kernel, ny, nx, nz),
        out_shape=jax.ShapeDtypeStruct((rows, width), BF16),
        in_specs=[any_space] * 3 + [pl.BlockSpec(memory_space=pltpu.SMEM)] + [any_space] * 5,
        out_specs=vmem,
        scratch_shapes=[
            pltpu.VMEM((rows, width), BF16),
            pltpu.VMEM((2 * ny, 4, width // (2 * ny), width), BF16),
            pltpu.VMEM((nt, keys_dev, width), BF16),
            pltpu.VMEM((width // 128, keys, 128), F32),
            pltpu.VMEM((slots, regions), jnp.int32),
            pltpu.VMEM((slots, regions), jnp.int32),
            pltpu.VMEM((width,), F32),
            pltpu.VMEM((2, slots, regions), jnp.int32),
            pltpu.VMEM((2, slots, regions), jnp.int32),
            pltpu.VMEM((keys_dev, width), F32),
            pltpu.VMEM((2, keys_dev, width), F32),
            pltpu.VMEM((2, keys_dev, width), F32),
            pltpu.VMEM((2, HEADS // 2, 256, rows), BF16),
            pltpu.VMEM((2, keys // 2, width), BF16),
            pltpu.VMEM((2, width, keys // 2), BF16),
            pltpu.VMEM((width, rows), BF16),
            pltpu.VMEM((width, width), BF16),
            dma((8,)),
            dma((3, 2)),
            dma((3, 2)),
            dma((2,)),
            dma((2, 4)),
            dma((2, 4)),
            dma((2,)),
            dma((2,)),
            dma,
            dma((nz,)),
            dma,
            dma,
            pltpu.SemaphoreType.REGULAR((nz,)),
        ],
        compiler_params=pltpu.CompilerParams(
            collective_id=0, has_side_effects=True, vmem_limit_bytes=24 * 1024 * 1024
        ),
        name="dilated_attention",
    )(*(keep(a) for a in (tiles[0], idx, msk)), tile_count, *(keep(a) for a in (w_query, w_key, w_value, w_out, key_gain)))
    return out[None]


def solution(mesh, nz=NZ):
    ny = mesh.shape["fsdp"] // 2
    nx = mesh.shape["tile"] // nz
    placed = (
        P("fsdp", "tile", None),
        P("fsdp", "tile", None),
        P("fsdp", "tile", None),
        P("fsdp"),
        P("fsdp", None),
        P("fsdp", None),
        P("fsdp", None),
        P("fsdp", None),
        P(),
    )
    return jax.shard_map(
        functools.partial(body, ny, nx, nz),
        mesh=mesh, in_specs=placed, out_specs=P("fsdp", "tile", None), check_vma=False,
    )
```

```python
import functools
import math

import jax
import jax.numpy as jnp
from jax import lax
from jax.experimental import pallas as pl
from jax.experimental.pallas import tpu as pltpu
from jax.sharding import PartitionSpec as P

HEADS = 16
REGIONS_PER_KEY = 8
TILES_PER_KEY = 32
NZ = 16
MESH = pl.DeviceIdType.MESH
BF16 = jnp.bfloat16
GROUPS = ((0,), (1, 2, 3), (4, 5, 6, 7), (8, 9, 10, 11), (12, 13, 14), (15,))
F32 = jnp.float32
WINDOWS = ((0, 128), (0, 128), (0, 256), (128, 128), (128, 128), (128, 256), (256, 128), (256, 128))


def pooling_weights(idx, msk, base, rows):
    m = msk.astype(F32)
    share = m / jnp.maximum(jnp.sum(m, axis=0, keepdims=True), 1.0)
    at = idx - base
    slots, regions = idx.shape
    tile = lax.broadcasted_iota(jnp.int32, (rows, regions), 0)
    acc = jnp.zeros((rows, regions), F32)
    for s in range(slots):
        acc = acc + jnp.where(tile == at[s : s + 1, :], share[s : s + 1, :], 0.0)
    acc = acc.T
    keys = regions // REGIONS_PER_KEY
    return jnp.sum(acc.reshape(keys, REGIONS_PER_KEY, rows), axis=1) * (1.0 / REGIONS_PER_KEY)


def exact_dot(w, x):
    hi = w.astype(BF16)
    rest = w - hi.astype(F32)
    mid = rest.astype(BF16)
    low = (rest - mid.astype(F32)).astype(BF16)
    n = w.shape[0]
    parts = jnp.concatenate([hi.astype(F32), mid.astype(F32), low.astype(F32)], axis=0).astype(BF16)
    y = jnp.dot(parts, x, preferred_element_type=F32)
    return y[:n] + y[n : 2 * n] + y[2 * n :]


STARTS = (0.0, 2.6, 5.0, 5.2, 7.3, 8.8, 10.3, 10.0, 12.7, 12.7, 14.8, 15.7, 15.2, 16.2, 18.0, 15.9)
LATE_RING = 13.0
SLACK = 4.0
RELAYS = ((0, 1), (1, 1), (0, 2), (1, 2), (0, 3), (1, 3), (0, 4), (1, 4))


def chunks(nz):
    if nz == len(STARTS):
        return ((0, 1), (1, 5), (5, 9), (9, 13), (13, 16))
    return ((0, 1), (1, nz // 2 + 1), (nz // 2 + 1, nz))


def expected(nz, ring_from=0.0):
    start = [STARTS[z * (len(STARTS) - 1) // max(nz - 1, 1)] for z in range(nz)]

    def dist(a, b):
        d = abs(a - b)
        return min(d, nz - d)

    def data(d):
        return 0.9 + 0.77 * d

    def signal(d):
        return 0.25 + 0.7 * d

    ready = [max(start[max(z - 1, 0) : z + 2]) + 2.0 for z in range(nz)]
    up = ready
    last = nz - 1
    arrive = {}
    for z in range(nz):
        if z > 0:
            arrive[z, 0] = max(ready[z], ready[z - 1] + data(1))
        if z < last:
            arrive[z, 1] = max(ready[z], ready[z + 1] + data(1))
    arrive[0, 0] = up[last] + data(2)
    arrive[last, 1] = arrive[0, 0] + data(2)
    part = {k: v + 0.6 for k, v in arrive.items()}
    norm = []
    for z in range(nz):
        left = part[z - 1, 1] + data(1) if z > 0 else part[last, 1] + data(2)
        right = part[z + 1, 0] + data(1) if z < last else part[0, 0] + data(2)
        norm.append(max(left, right, up[z], part[z, 0], part[z, 1]) + 0.3)
    sent = {}
    for z in range(nz):
        for e in range(1, nz):
            to = z + e
            sent[z, e] = norm[z] if to >= nz else max(norm[z], up[to] + signal(dist(z, to)))
    plans = []
    for z in range(nz):
        p = [(arrive[z, 0], "part", 0), (arrive[z, 1], "part", 1), (norm[z], "norm", None)]
        for i, ws in enumerate(RELAYS):
            alone = ring_from > 0.0 and z == 0
            pace = 2.2 if alone else 3.4
            tm = max(ready[z], ring_from) + 1.7 + pace * (i + 1 if i < 6 else 7)
            close = 1.5 if alone else 3.0
            p.append((norm[z] + 1.1 + 0.01 * i if norm[z] - close < tm < norm[z] + 1.0 else tm, "relay", ws))
        for e in range(1, nz):
            if z + e < nz:
                p.append((sent[z, e] + 1.0, "zsend", z + e))
            src = (z - e) % nz
            p.append((sent[src, e] + data(dist(z, src)) + SLACK, "zarr", src))
        got = {src: tm for tm, kind, src in p if kind == "zarr"}
        got[z] = norm[z]
        for lo, hi in chunks(nz):
            p.append((max(got[src] for src in range(lo, hi)), "xsend", (lo, hi)))
        plans.append(p)
    return plans


def orders(nz):
    out = []
    for members in GROUPS if nz == len(STARTS) else tuple((z,) for z in range(nz)):
        if STARTS[members[0]] < LATE_RING:
            out.append((members, (0,), order_of(members, expected(nz, LATE_RING))))
            out.append((members, (1, 2, 3), order_of(members, expected(nz))))
        else:
            out.append((members, (0, 1, 2, 3), order_of(members, expected(nz))))
    return out


def in_first_half(kind, arg, nz):
    if kind == "zarr":
        return 1 <= arg <= nz // 2
    return kind == "xsend" and 1 <= arg[0] and arg[1] <= nz // 2 + 1


def order_of(members, plans):
    when = {}
    for z in members:
        for tm, kind, arg in plans[z]:
            when[kind, arg] = max(tm, when.get((kind, arg), 0.0))
    done = when["norm", None]
    when = {k: max(tm, done + 0.01) if k[0] in ("zsend", "xsend") else tm for k, tm in when.items()}
    cuts = [-1.0] + [max(when["relay", (b, s)] for s in range(1, 5)) + 0.9 + b for b in (0, 1)] + [1e9]
    first = [tm for (kind, arg), tm in when.items() if in_first_half(kind, arg, len(plans))]
    cuts[2] = max([cuts[2]] + [tm + 0.001 for tm in first])
    listed = sorted(when.items(), key=lambda it: it[1])
    return [[k for k, tm in listed if lo < tm <= hi] for lo, hi in zip(cuts[:-1], cuts[1:])]


def kernel(
    ny, nx, nz,
    tiles_hbm, idx_hbm, msk_hbm, cnt_ref, wq_hbm, wk_hbm, wv_hbm, wo_hbm, gain_hbm,
    out_ref,
    tiles_v, w_v, ng, nf, oidx, omsk, ogain, nidx, nmsk, pown, pout, pin, qz, kk, vt, ctxt, wvt, tops, totals, accs,
    loc_sem, halo_send, halo_recv, ring_send, ring_r, ring_l, pair_send, pair_recv, z_send, z_recv, x_send, x_recv,
    here_sem,
):
    f = lax.axis_index("fsdp")
    t = lax.axis_index("tile")
    nt = nx * nz
    y = f // 2
    core = f % 2
    xx = t // nz
    zz = t % nz
    w_hbm = (wq_hbm, wk_hbm, wv_hbm, wo_hbm)
    sh = wq_hbm.shape[0]
    rows, width = tiles_hbm.shape
    hd = width // HEADS
    half = HEADS // 2
    bl = half * hd

    def at_y(d):
        return (((y + d + ny) % ny) * 2 + core, t)

    def at_z(d):
        return (f, xx * nz + (zz + d + nz) % nz)

    def at_x(d):
        return (f, ((xx + d + nx) % nx) * nz + zz)

    def at_t(d):
        return (f, (t + d + nt) % nt)

    pair = (y * 2 + 1 - core, t)

    barrier = pltpu.get_barrier_semaphore()

    def greet(dev, sem=barrier):
        pl.semaphore_signal(sem, inc=1, device_id=dev, device_id_type=MESH)

    near = [pair]
    near += [at_y(d) for d in ((1, -1) if ny > 1 else ())]
    near += [at_x(d) for d in range(1, nx)]
    for p in near:
        greet(p)
    is_first = zz == 0
    is_last = zz == nz - 1

    @pl.when(jnp.logical_not(is_first))
    def _():
        greet(at_z(-1))

    @pl.when(is_first)
    def _():
        greet(at_t(-1))

    for k in range(1, nz):
        @pl.when(zz + k < nz)
        def _(k=k):
            greet(at_z(k))

    loads = [
        pltpu.make_async_copy(src, dst, loc_sem.at[i])
        for i, (src, dst) in enumerate(
            [(tiles_hbm, tiles_v), (idx_hbm, oidx), (msk_hbm, omsk), (gain_hbm, ogain)]
            + [(w_hbm[w], w_v.at[f, w]) for w in range(4)]
        )
    ]
    for c in loads:
        c.start()
    own_loads = loads[4:]
    pl.semaphore_wait(barrier, len(near) + zz + 1)

    def remote(src, dst, send, recv, dev):
        return pltpu.make_async_remote_copy(
            src_ref=src, dst_ref=dst, send_sem=send, recv_sem=recv, device_id=dev, device_id_type=MESH
        )

    def arrived(dst, sem):
        pltpu.make_async_copy(dst, dst, sem).wait()

    def lists_to(d):
        slot = 0 if d == 1 else 1
        remote(idx_hbm, nidx.at[slot], halo_send.at[0, slot], halo_recv.at[0, slot], at_t(d)).start()
        remote(msk_hbm, nmsk.at[slot], halo_send.at[1, slot], halo_recv.at[1, slot], at_t(d)).start()

    steps_r = [(ny - 1) // 2 + (1 if ny % 2 == 0 and b % 2 == 0 else 0) for b in range(2)]
    steps_l = [(ny - 1) // 2 + (1 if ny % 2 == 0 and b % 2 == 1 else 0) for b in range(2)]

    def slot_of(b, owner_d):
        return w_v.at[((y + owner_d + ny) % ny) * 2 + core, pl.ds(2 * b, 2)]

    def pass_on(b, owner_d):
        ref = slot_of(b, owner_d)
        remote(ref, ref, pair_send.at[b], pair_recv.at[b], pair).start()

    def ring_start(b, s, right):
        ref = slot_of(b, -(s - 1) if right else s - 1)
        sem = (ring_r if right else ring_l).at[b, s - 1]
        remote(ref, ref, ring_send.at[b], sem, at_y(1 if right else -1)).start()

    def relay(b, s):
        if steps_r[b] >= s:
            arrived(slot_of(b, -s), ring_r.at[b, s - 1])
            if steps_r[b] > s:
                ring_start(b, s + 1, True)
            pass_on(b, -s)
        if steps_l[b] >= s:
            arrived(slot_of(b, s), ring_l.at[b, s - 1])
            if steps_l[b] > s:
                ring_start(b, s + 1, False)
            pass_on(b, s)

    def complete(b):
        arrived(w_v.at[pl.ds(0, ny), pl.ds(2 * b, 2)], pair_recv.at[b])

    def weight(w):
        return w_v[:, w].reshape(width, width)

    lists_to(1)

    @pl.when(jnp.logical_not(is_first))
    def _():
        lists_to(-1)

    for k in range(1, nz):
        @pl.when(k <= zz)
        def _(k=k):
            greet(at_z(-k), here_sem.at[zz])

    for b in range(2):
        for c in own_loads[2 * b : 2 * b + 2]:
            c.wait()
        if steps_r[b] >= 1:
            ring_start(b, 1, True)
        if steps_l[b] >= 1:
            ring_start(b, 1, False)
    for b in range(2):
        pass_on(b, 0)

    base = t * rows
    for c in loads[:4]:
        c.wait()
    pown[...] = exact_dot(pooling_weights(oidx[...], omsk[...], base, rows), tiles_v[...])

    def part(slot):
        d = -1 if slot == 0 else 1
        arrived(nidx.at[slot], halo_recv.at[0, slot])
        arrived(nmsk.at[slot], halo_recv.at[1, slot])
        if slot == 0:
            @pl.when(is_first)
            def _():
                lists_to(-1)

        wts = pooling_weights(nidx[slot], nmsk[slot], base, rows)
        pout[slot] = exact_dot(wts, tiles_v[...])
        remote(pout.at[slot], pin.at[1 - slot], halo_send.at[2, slot], halo_recv.at[2, 1 - slot], at_t(d)).start()

    def norm():
        for slot in (0, 1):
            arrived(pin.at[slot], halo_recv.at[2, slot])
        pooled = pown[...] + pin[0] + pin[1]
        scale = lax.rsqrt(jnp.mean(pooled * pooled, axis=1, keepdims=True) + 1e-06)
        ng[t] = (pooled * scale * ogain[...].reshape(1, width)).astype(BF16)
        for d in range(1, nz):
            e = ((d + 1) // 2 if d % 2 else -(d // 2)) % nz

            @pl.when(zz + e >= nz)
            def _(e=e):
                z_block(zz + e - nz)


    def z_block(to):
        remote(ng.at[t], ng.at[t], z_send, z_recv.at[zz], (f, xx * nz + to)).start()

    def zsend(to):
        @pl.when(to > zz)
        def _():
            pl.semaphore_wait(here_sem.at[to], 1)
            z_block(to)

    def xsend(span):
        lo, hi = span
        block = ng.at[pl.ds(xx * nz + lo, hi - lo)]
        for d in range(1, nx):
            sem = x_recv.at[0 if in_first_half("xsend", span, nz) else 1]
            remote(block, block, x_send, sem, at_x(d)).start()

    def zarr(src):
        @pl.when(src != zz)
        def _():
            arrived(ng.at[xx * nz + src], z_recv.at[src])

    handlers = {
        "part": part, "norm": lambda _: norm(), "relay": lambda ws: relay(*ws),
        "zsend": zsend, "zarr": zarr, "xsend": xsend,
    }
    listed = orders(nz)

    def run(stage):
        for members, columns, stages in listed:
            rows_in = jnp.logical_and(zz >= members[0], zz <= members[-1])

            @pl.when(jnp.logical_and(rows_in, jnp.logical_and(xx >= columns[0], xx <= columns[-1])))
            def _(todo=stages[stage]):
                for kind, arg in todo:
                    handlers[kind](arg)

    def query():
        complete(0)
        q = jnp.dot(tiles_v[...], weight(0), preferred_element_type=F32)
        qt = q.T.astype(BF16)
        qz[...] = jnp.zeros(qz.shape, BF16)
        for h in range(HEADS):
            g, i = divmod(h, half)
            lo = hd * i - WINDOWS[i][0]
            qz[g, i, lo : lo + hd, :] = qt[h * hd : (h + 1) * hd, :]

    def value_weights():
        complete(1)
        wvt[...] = weight(2).T

    def attend(half_at):
        rows_z = nz // 2
        if nx > 1:
            arrived(ng.at[pl.ds(0, rows_z * (nx - 1))], x_recv.at[half_at])
        blocks = []
        for x in range(nx):
            at = x * nz
            blocks += [ng[at + 1 : at + 1 + rows_z]] if half_at == 0 else [ng[at : at + 1], ng[at + 1 + rows_z : at + nz]]
        every = jnp.concatenate([b.astype(F32).reshape(-1, width) for b in blocks], axis=0)
        for j in range(nf.shape[0]):
            nf[j] = every[:, j * 128 : (j + 1) * 128]
        n_par = nf.shape[1] // 2
        for par in (0, 1):
            n = [nf[j, pl.ds(par, n_par, stride=2), :] for j in range(nf.shape[0])]
            n = jnp.concatenate(n, axis=1).astype(BF16)
            kk[par] = jnp.dot(n, weight(1), preferred_element_type=F32).astype(BF16)
            vt[par] = lax.dot_general(
                wvt[...], n, (((1,), (1,)), ((), ())), preferred_element_type=F32
            ).astype(BF16)
        count = cnt_ref[0]
        factor = math.log2(math.e) / math.sqrt(hd)
        at = lax.broadcasted_iota(jnp.int32, (n_par, rows), 0)
        keys_z = ng.shape[1]
        per_x = rows_z * keys_z // 2
        within = 2 * (at % per_x)
        if half_at == 0:
            within = within + keys_z
        else:
            within = within + jnp.where(within >= keys_z, rows_z * keys_z, 0)
        position = ((at // per_x) * (nz * keys_z) + within) * TILES_PER_KEY

        @pl.loop(0, 2)
        def _(g):
            for i in range(half):
                par = i % 2
                valid = position + par * TILES_PER_KEY < count
                lo, wide = WINDOWS[i]
                lanes = pl.ds(pl.multiple_of(g * bl + lo, 128), wide)
                score = jnp.dot(kk[par, :, lanes], qz[g, i, :wide, :], preferred_element_type=F32)
                score = jnp.where(valid, score, -jnp.inf)
                top = jnp.max(score, axis=0, keepdims=True)
                weights = jnp.exp2((score - top) * factor)
                total = jnp.sum(weights, axis=0, keepdims=True)
                h = g * half + i
                head = pl.ds(pl.multiple_of(g * bl + i * hd, 16), hd)
                acc = jnp.dot(vt[par, head, :], weights.astype(BF16), preferred_element_type=F32)
                if half_at == 0:
                    tops[h] = top
                    totals[h] = total
                    accs[head, :] = acc
                else:
                    old = tops[h]
                    best = jnp.maximum(old, top)
                    f_old = jnp.exp2((old - best) * factor)
                    f_new = jnp.exp2((top - best) * factor)
                    total = totals[h] * f_old + total * f_new
                    ctxt[head, :] = ((accs[head, :] * f_old + acc * f_new) / total).astype(BF16)

    def project():
        out_ref[...] = jnp.dot(ctxt[...].T, weight(3), preferred_element_type=F32).astype(BF16)

    run(0)
    query()
    run(1)
    value_weights()
    attend(0)
    run(2)
    attend(1)
    project()

    for slot in (0, 1):
        arrived(nidx.at[slot], halo_send.at[0, slot])
        arrived(nmsk.at[slot], halo_send.at[1, slot])
        arrived(pout.at[slot], halo_send.at[2, slot])
    for b in range(2):
        arrived(w_v.at[pl.ds(0, ny), pl.ds(2 * b, 2)], pair_send.at[b])
        if ny > 1:
            arrived(w_v.at[pl.ds(0, ny - 1), pl.ds(2 * b, 2)], ring_send.at[b])
    arrived(ng.at[pl.ds(0, nz - 1)], z_send)
    if nx > 1:
        arrived(ng.at[pl.ds(0, nz * (nx - 1))], x_send)


def body(ny, nx, nz, tiles, nbr_tiles, nbr_mask, tile_count, w_query, w_key, w_value, w_out, key_gain):
    rows, width = tiles.shape[1:]
    idx = jnp.transpose(nbr_tiles[0])
    msk = jnp.transpose(nbr_mask[0])
    slots, regions = idx.shape
    keys_dev = regions // REGIONS_PER_KEY
    nt = nx * nz
    keys = keys_dev * nt
    keep = functools.partial(pltpu.with_memory_space_constraint, memory_space=pltpu.HBM)
    any_space = pl.BlockSpec(memory_space=pl.ANY)
    vmem = pl.BlockSpec(memory_space=pltpu.VMEM)
    dma = pltpu.SemaphoreType.DMA
    out = pl.pallas_call(
        functools.partial(kernel, ny, nx, nz),
        out_shape=jax.ShapeDtypeStruct((rows, width), BF16),
        in_specs=[any_space] * 3 + [pl.BlockSpec(memory_space=pltpu.SMEM)] + [any_space] * 5,
        out_specs=vmem,
        scratch_shapes=[
            pltpu.VMEM((rows, width), BF16),
            pltpu.VMEM((2 * ny, 4, width // (2 * ny), width), BF16),
            pltpu.VMEM((nt, keys_dev, width), BF16),
            pltpu.VMEM((width // 128, keys // 2, 128), F32),
            pltpu.VMEM((slots, regions), jnp.int32),
            pltpu.VMEM((slots, regions), jnp.int32),
            pltpu.VMEM((width,), F32),
            pltpu.VMEM((2, slots, regions), jnp.int32),
            pltpu.VMEM((2, slots, regions), jnp.int32),
            pltpu.VMEM((keys_dev, width), F32),
            pltpu.VMEM((2, keys_dev, width), F32),
            pltpu.VMEM((2, keys_dev, width), F32),
            pltpu.VMEM((2, HEADS // 2, 256, rows), BF16),
            pltpu.VMEM((2, keys // 4, width), BF16),
            pltpu.VMEM((2, width, keys // 4), BF16),
            pltpu.VMEM((width, rows), BF16),
            pltpu.VMEM((width, width), BF16),
            pltpu.VMEM((HEADS, 1, rows), F32),
            pltpu.VMEM((HEADS, 1, rows), F32),
            pltpu.VMEM((width, rows), F32),
            dma((8,)),
            dma((3, 2)),
            dma((3, 2)),
            dma((2,)),
            dma((2, 4)),
            dma((2, 4)),
            dma((2,)),
            dma((2,)),
            dma,
            dma((nz,)),
            dma,
            dma((2,)),
            pltpu.SemaphoreType.REGULAR((nz,)),
        ],
        compiler_params=pltpu.CompilerParams(
            collective_id=0, has_side_effects=True, vmem_limit_bytes=24 * 1024 * 1024
        ),
        name="dilated_attention",
    )(*(keep(a) for a in (tiles[0], idx, msk)), tile_count, *(keep(a) for a in (w_query, w_key, w_value, w_out, key_gain)))
    return out[None]


def solution(mesh, nz=NZ):
    ny = mesh.shape["fsdp"] // 2
    nx = mesh.shape["tile"] // nz
    placed = (
        P("fsdp", "tile", None),
        P("fsdp", "tile", None),
        P("fsdp", "tile", None),
        P("fsdp"),
        P("fsdp", None),
        P("fsdp", None),
        P("fsdp", None),
        P("fsdp", None),
        P(),
    )
    return jax.shard_map(
        functools.partial(body, ny, nx, nz),
        mesh=mesh, in_specs=placed, out_specs=P("fsdp", "tile", None), check_vma=False,
    )
```

```python
import functools
import math

import jax
import jax.numpy as jnp
from jax import lax
from jax.experimental import pallas as pl
from jax.experimental.pallas import tpu as pltpu
from jax.sharding import PartitionSpec as P

HEADS = 16
REGIONS_PER_KEY = 8
TILES_PER_KEY = 32
NZ = 16
MESH = pl.DeviceIdType.MESH
BF16 = jnp.bfloat16
GROUPS = ((0,), (1, 2, 3), (4, 5, 6, 7), (8, 9, 10, 11), (12, 13, 14), (15,))
F32 = jnp.float32
WINDOWS = ((0, 128), (0, 128), (0, 256), (128, 128), (128, 128), (128, 256), (256, 128), (256, 128))


def pooling_weights(idx, msk, base, rows):
    m = msk.astype(F32)
    share = m / jnp.maximum(jnp.sum(m, axis=0, keepdims=True), 1.0)
    at = idx - base
    slots, regions = idx.shape
    tile = lax.broadcasted_iota(jnp.int32, (rows, regions), 0)
    acc = jnp.zeros((rows, regions), F32)
    for s in range(slots):
        acc = acc + jnp.where(tile == at[s : s + 1, :], share[s : s + 1, :], 0.0)
    acc = acc.T
    keys = regions // REGIONS_PER_KEY
    return jnp.sum(acc.reshape(keys, REGIONS_PER_KEY, rows), axis=1) * (1.0 / REGIONS_PER_KEY)


def exact_dot(w, x):
    hi = w.astype(BF16)
    rest = w - hi.astype(F32)
    mid = rest.astype(BF16)
    low = (rest - mid.astype(F32)).astype(BF16)
    n = w.shape[0]
    parts = jnp.concatenate([hi.astype(F32), mid.astype(F32), low.astype(F32)], axis=0).astype(BF16)
    y = jnp.dot(parts, x, preferred_element_type=F32)
    return y[:n] + y[n : 2 * n] + y[2 * n :]


STARTS = (0.0, 2.6, 5.0, 5.2, 7.3, 8.8, 10.3, 10.0, 12.7, 12.7, 14.8, 15.7, 15.2, 16.2, 18.0, 15.9)
LATE_RING = 13.0
SLACK = 4.0
RELAYS = ((0, 1), (1, 1), (0, 2), (1, 2), (0, 3), (1, 3), (0, 4), (1, 4))


def chunks(nz):
    if nz == len(STARTS):
        return ((0, 1), (1, 5), (5, 9), (9, 13), (13, 16))
    return ((0, 1), (1, nz // 2 + 1), (nz // 2 + 1, nz))


def expected(nz, ring_from=0.0):
    start = [STARTS[z * (len(STARTS) - 1) // max(nz - 1, 1)] for z in range(nz)]

    def dist(a, b):
        d = abs(a - b)
        return min(d, nz - d)

    def data(d):
        return 0.9 + 0.77 * d

    def signal(d):
        return 0.25 + 0.7 * d

    ready = [max(start[max(z - 1, 0) : z + 2]) + 2.0 for z in range(nz)]
    up = ready
    last = nz - 1
    arrive = {}
    for z in range(nz):
        if z > 0:
            arrive[z, 0] = max(ready[z], ready[z - 1] + data(1))
        if z < last:
            arrive[z, 1] = max(ready[z], ready[z + 1] + data(1))
    arrive[0, 0] = up[last] + data(2)
    arrive[last, 1] = arrive[0, 0] + data(2)
    part = {k: v + 0.6 for k, v in arrive.items()}
    norm = []
    for z in range(nz):
        left = part[z - 1, 1] + data(1) if z > 0 else part[last, 1] + data(2)
        right = part[z + 1, 0] + data(1) if z < last else part[0, 0] + data(2)
        norm.append(max(left, right, up[z], part[z, 0], part[z, 1]) + 0.3)
    sent = {}
    for z in range(nz):
        for e in range(1, nz):
            to = z + e
            sent[z, e] = norm[z] if to >= nz else max(norm[z], up[to] + signal(dist(z, to)))
    plans = []
    for z in range(nz):
        p = [(arrive[z, 0], "part", 0), (arrive[z, 1], "part", 1), (norm[z], "norm", None)]
        for i, ws in enumerate(RELAYS):
            alone = ring_from > 0.0 and z == 0
            pace = 2.2 if alone else 3.4
            tm = max(ready[z], ring_from) + 1.7 + pace * (i + 1 if i < 6 else 7)
            close = 1.5 if alone else 3.0
            p.append((norm[z] + 1.1 + 0.01 * i if norm[z] - close < tm < norm[z] + 1.0 else tm, "relay", ws))
        for e in range(1, nz):
            if z + e < nz:
                p.append((sent[z, e] + 1.0, "zsend", z + e))
            src = (z - e) % nz
            p.append((sent[src, e] + data(dist(z, src)) + (SLACK if z > 7 else 5.5), "zarr", src))
        got = {src: tm for tm, kind, src in p if kind == "zarr"}
        got[z] = norm[z]
        for lo, hi in chunks(nz):
            p.append((max(got[src] for src in range(lo, hi)), "xsend", (lo, hi)))
        plans.append(p)
    return plans


def orders(nz):
    out = []
    for members in GROUPS if nz == len(STARTS) else tuple((z,) for z in range(nz)):
        if STARTS[members[0]] < LATE_RING:
            out.append((members, (0,), order_of(members, expected(nz, LATE_RING))))
            out.append((members, (1, 2, 3), order_of(members, expected(nz))))
        else:
            out.append((members, (0, 1, 2, 3), order_of(members, expected(nz))))
    return out


def in_first_half(kind, arg, nz):
    if kind == "zarr":
        return 1 <= arg <= nz // 2
    return kind == "xsend" and 1 <= arg[0] and arg[1] <= nz // 2 + 1


def order_of(members, plans):
    when = {}
    for z in members:
        for tm, kind, arg in plans[z]:
            when[kind, arg] = max(tm, when.get((kind, arg), 0.0))
    done = when["norm", None]
    when = {k: max(tm, done + 0.01) if k[0] in ("zsend", "xsend") else tm for k, tm in when.items()}
    cuts = [-1.0] + [max(when["relay", (b, s)] for s in range(1, 5)) + 0.9 + b for b in (0, 1)] + [1e9]
    first = [tm for (kind, arg), tm in when.items() if in_first_half(kind, arg, len(plans))]
    cuts[2] = max([cuts[2]] + [tm + 0.001 for tm in first])
    listed = sorted(when.items(), key=lambda it: it[1])
    return [[k for k, tm in listed if lo < tm <= hi] for lo, hi in zip(cuts[:-1], cuts[1:])]


def kernel(
    ny, nx, nz,
    tiles_hbm, idx_hbm, msk_hbm, cnt_ref, wq_hbm, wk_hbm, wv_hbm, wo_hbm, gain_hbm,
    out_ref,
    tiles_v, w_v, ng, nf, oidx, omsk, ogain, nidx, nmsk, pown, pout, pin, qz, kk, vt, ctxt, wvt, tops, totals, accs,
    loc_sem, halo_send, halo_recv, ring_send, ring_r, ring_l, pair_send, pair_recv, z_send, z_recv, x_send, x_recv,
    here_sem,
):
    f = lax.axis_index("fsdp")
    t = lax.axis_index("tile")
    nt = nx * nz
    y = f // 2
    core = f % 2
    xx = t // nz
    zz = t % nz
    w_hbm = (wq_hbm, wk_hbm, wv_hbm, wo_hbm)
    sh = wq_hbm.shape[0]
    rows, width = tiles_hbm.shape
    hd = width // HEADS
    half = HEADS // 2
    bl = half * hd

    def at_y(d):
        return (((y + d + ny) % ny) * 2 + core, t)

    def at_z(d):
        return (f, xx * nz + (zz + d + nz) % nz)

    def at_x(d):
        return (f, ((xx + d + nx) % nx) * nz + zz)

    def at_t(d):
        return (f, (t + d + nt) % nt)

    pair = (y * 2 + 1 - core, t)

    barrier = pltpu.get_barrier_semaphore()

    def greet(dev, sem=barrier):
        pl.semaphore_signal(sem, inc=1, device_id=dev, device_id_type=MESH)

    near = [pair]
    near += [at_y(d) for d in ((1, -1) if ny > 1 else ())]
    near += [at_x(d) for d in range(1, nx)]
    for p in near:
        greet(p)
    is_first = zz == 0
    is_last = zz == nz - 1

    @pl.when(jnp.logical_not(is_first))
    def _():
        greet(at_z(-1))

    @pl.when(is_first)
    def _():
        greet(at_t(-1))

    for k in range(1, nz):
        @pl.when(zz + k < nz)
        def _(k=k):
            greet(at_z(k))

    loads = [
        pltpu.make_async_copy(src, dst, loc_sem.at[i])
        for i, (src, dst) in enumerate(
            [(tiles_hbm, tiles_v), (idx_hbm, oidx), (msk_hbm, omsk), (gain_hbm, ogain)]
            + [(w_hbm[w], w_v.at[f, w]) for w in range(4)]
        )
    ]
    for c in loads:
        c.start()
    own_loads = loads[4:]
    pl.semaphore_wait(barrier, len(near) + zz + 1)

    def remote(src, dst, send, recv, dev):
        return pltpu.make_async_remote_copy(
            src_ref=src, dst_ref=dst, send_sem=send, recv_sem=recv, device_id=dev, device_id_type=MESH
        )

    def arrived(dst, sem):
        pltpu.make_async_copy(dst, dst, sem).wait()

    def lists_to(d):
        slot = 0 if d == 1 else 1
        remote(idx_hbm, nidx.at[slot], halo_send.at[0, slot], halo_recv.at[0, slot], at_t(d)).start()
        remote(msk_hbm, nmsk.at[slot], halo_send.at[1, slot], halo_recv.at[1, slot], at_t(d)).start()

    steps_r = [(ny - 1) // 2 + (1 if ny % 2 == 0 and b % 2 == 0 else 0) for b in range(2)]
    steps_l = [(ny - 1) // 2 + (1 if ny % 2 == 0 and b % 2 == 1 else 0) for b in range(2)]

    def slot_of(b, owner_d):
        return w_v.at[((y + owner_d + ny) % ny) * 2 + core, pl.ds(2 * b, 2)]

    def pass_on(b, owner_d):
        ref = slot_of(b, owner_d)
        remote(ref, ref, pair_send.at[b], pair_recv.at[b], pair).start()

    def ring_start(b, s, right):
        ref = slot_of(b, -(s - 1) if right else s - 1)
        sem = (ring_r if right else ring_l).at[b, s - 1]
        remote(ref, ref, ring_send.at[b], sem, at_y(1 if right else -1)).start()

    def relay(b, s):
        if steps_r[b] >= s:
            arrived(slot_of(b, -s), ring_r.at[b, s - 1])
            if steps_r[b] > s:
                ring_start(b, s + 1, True)
            pass_on(b, -s)
        if steps_l[b] >= s:
            arrived(slot_of(b, s), ring_l.at[b, s - 1])
            if steps_l[b] > s:
                ring_start(b, s + 1, False)
            pass_on(b, s)

    def complete(b):
        arrived(w_v.at[pl.ds(0, ny), pl.ds(2 * b, 2)], pair_recv.at[b])

    def weight(w):
        return w_v[:, w].reshape(width, width)

    lists_to(1)

    @pl.when(jnp.logical_not(is_first))
    def _():
        lists_to(-1)

    for k in range(1, nz):
        @pl.when(k <= zz)
        def _(k=k):
            greet(at_z(-k), here_sem.at[zz])

    for b in range(2):
        for c in own_loads[2 * b : 2 * b + 2]:
            c.wait()
        if steps_r[b] >= 1:
            ring_start(b, 1, True)
        if steps_l[b] >= 1:
            ring_start(b, 1, False)
    for b in range(2):
        pass_on(b, 0)

    base = t * rows
    for c in loads[:4]:
        c.wait()
    pown[...] = exact_dot(pooling_weights(oidx[...], omsk[...], base, rows), tiles_v[...])

    def part(slot):
        d = -1 if slot == 0 else 1
        arrived(nidx.at[slot], halo_recv.at[0, slot])
        arrived(nmsk.at[slot], halo_recv.at[1, slot])
        if slot == 0:
            @pl.when(is_first)
            def _():
                lists_to(-1)

        wts = pooling_weights(nidx[slot], nmsk[slot], base, rows)
        pout[slot] = exact_dot(wts, tiles_v[...])
        remote(pout.at[slot], pin.at[1 - slot], halo_send.at[2, slot], halo_recv.at[2, 1 - slot], at_t(d)).start()

    def norm():
        for slot in (0, 1):
            arrived(pin.at[slot], halo_recv.at[2, slot])
        pooled = pown[...] + pin[0] + pin[1]
        scale = lax.rsqrt(jnp.mean(pooled * pooled, axis=1, keepdims=True) + 1e-06)
        ng[t] = (pooled * scale * ogain[...].reshape(1, width)).astype(BF16)
        for d in range(1, nz):
            e = ((d + 1) // 2 if d % 2 else -(d // 2)) % nz

            @pl.when(zz + e >= nz)
            def _(e=e):
                z_block(zz + e - nz)


    def z_block(to):
        remote(ng.at[t], ng.at[t], z_send, z_recv.at[zz], (f, xx * nz + to)).start()

    def zsend(to):
        @pl.when(to > zz)
        def _():
            pl.semaphore_wait(here_sem.at[to], 1)
            z_block(to)

    def xsend(span):
        lo, hi = span
        block = ng.at[pl.ds(xx * nz + lo, hi - lo)]
        for d in range(1, nx):
            sem = x_recv.at[0 if in_first_half("xsend", span, nz) else 1]
            remote(block, block, x_send, sem, at_x(d)).start()

    def zarr(src):
        @pl.when(src != zz)
        def _():
            arrived(ng.at[xx * nz + src], z_recv.at[src])

    handlers = {
        "part": part, "norm": lambda _: norm(), "relay": lambda ws: relay(*ws),
        "zsend": zsend, "zarr": zarr, "xsend": xsend,
    }
    listed = orders(nz)

    def run(stage):
        for members, columns, stages in listed:
            rows_in = jnp.logical_and(zz >= members[0], zz <= members[-1])

            @pl.when(jnp.logical_and(rows_in, jnp.logical_and(xx >= columns[0], xx <= columns[-1])))
            def _(todo=stages[stage]):
                for kind, arg in todo:
                    handlers[kind](arg)

    def query():
        complete(0)
        q = jnp.dot(tiles_v[...], weight(0), preferred_element_type=F32)
        qt = q.T.astype(BF16)
        qz[...] = jnp.zeros(qz.shape, BF16)
        for h in range(HEADS):
            g, i = divmod(h, half)
            lo = hd * i - WINDOWS[i][0]
            qz[g, i, lo : lo + hd, :] = qt[h * hd : (h + 1) * hd, :]

    def value_weights():
        complete(1)
        wvt[...] = weight(2).T

    def attend(half_at):
        rows_z = nz // 2
        if nx > 1:
            arrived(ng.at[pl.ds(0, rows_z * (nx - 1))], x_recv.at[half_at])
        blocks = []
        for x in range(nx):
            at = x * nz
            blocks += [ng[at + 1 : at + 1 + rows_z]] if half_at == 0 else [ng[at : at + 1], ng[at + 1 + rows_z : at + nz]]
        every = jnp.concatenate([b.astype(F32).reshape(-1, width) for b in blocks], axis=0)
        for j in range(nf.shape[0]):
            nf[j] = every[:, j * 128 : (j + 1) * 128]
        n_par = nf.shape[1] // 2
        for par in (0, 1):
            n = [nf[j, pl.ds(par, n_par, stride=2), :] for j in range(nf.shape[0])]
            n = jnp.concatenate(n, axis=1).astype(BF16)
            kk[par] = jnp.dot(n, weight(1), preferred_element_type=F32).astype(BF16)
            vt[par] = lax.dot_general(
                wvt[...], n, (((1,), (1,)), ((), ())), preferred_element_type=F32
            ).astype(BF16)
        count = cnt_ref[0]
        factor = math.log2(math.e) / math.sqrt(hd)
        at = lax.broadcasted_iota(jnp.int32, (n_par, rows), 0)
        keys_z = ng.shape[1]
        per_x = rows_z * keys_z // 2
        within = 2 * (at % per_x)
        if half_at == 0:
            within = within + keys_z
        else:
            within = within + jnp.where(within >= keys_z, rows_z * keys_z, 0)
        position = ((at // per_x) * (nz * keys_z) + within) * TILES_PER_KEY

        @pl.loop(0, 2)
        def _(g):
            for i in range(half):
                par = i % 2
                valid = position + par * TILES_PER_KEY < count
                lo, wide = WINDOWS[i]
                lanes = pl.ds(pl.multiple_of(g * bl + lo, 128), wide)
                score = jnp.dot(kk[par, :, lanes], qz[g, i, :wide, :], preferred_element_type=F32)
                score = jnp.where(valid, score, -jnp.inf)
                top = jnp.max(score, axis=0, keepdims=True)
                weights = jnp.exp2((score - top) * factor)
                total = jnp.sum(weights, axis=0, keepdims=True)
                h = g * half + i
                head = pl.ds(pl.multiple_of(g * bl + i * hd, 16), hd)
                acc = jnp.dot(vt[par, head, :], weights.astype(BF16), preferred_element_type=F32)
                if half_at == 0:
                    tops[h] = top
                    totals[h] = total
                    accs[head, :] = acc
                else:
                    old = tops[h]
                    best = jnp.maximum(old, top)
                    f_old = jnp.exp2((old - best) * factor)
                    f_new = jnp.exp2((top - best) * factor)
                    total = totals[h] * f_old + total * f_new
                    ctxt[head, :] = ((accs[head, :] * f_old + acc * f_new) / total).astype(BF16)

    def project():
        out_ref[...] = jnp.dot(ctxt[...].T, weight(3), preferred_element_type=F32).astype(BF16)

    run(0)
    query()
    run(1)
    value_weights()
    attend(0)
    run(2)
    attend(1)
    project()

    for slot in (0, 1):
        arrived(nidx.at[slot], halo_send.at[0, slot])
        arrived(nmsk.at[slot], halo_send.at[1, slot])
        arrived(pout.at[slot], halo_send.at[2, slot])
    for b in range(2):
        arrived(w_v.at[pl.ds(0, ny), pl.ds(2 * b, 2)], pair_send.at[b])
        if ny > 1:
            arrived(w_v.at[pl.ds(0, ny - 1), pl.ds(2 * b, 2)], ring_send.at[b])
    arrived(ng.at[pl.ds(0, nz - 1)], z_send)
    if nx > 1:
        arrived(ng.at[pl.ds(0, nz * (nx - 1))], x_send)


def body(ny, nx, nz, tiles, nbr_tiles, nbr_mask, tile_count, w_query, w_key, w_value, w_out, key_gain):
    rows, width = tiles.shape[1:]
    idx = jnp.transpose(nbr_tiles[0])
    msk = jnp.transpose(nbr_mask[0])
    slots, regions = idx.shape
    keys_dev = regions // REGIONS_PER_KEY
    nt = nx * nz
    keys = keys_dev * nt
    keep = functools.partial(pltpu.with_memory_space_constraint, memory_space=pltpu.HBM)
    any_space = pl.BlockSpec(memory_space=pl.ANY)
    vmem = pl.BlockSpec(memory_space=pltpu.VMEM)
    dma = pltpu.SemaphoreType.DMA
    out = pl.pallas_call(
        functools.partial(kernel, ny, nx, nz),
        out_shape=jax.ShapeDtypeStruct((rows, width), BF16),
        in_specs=[any_space] * 3 + [pl.BlockSpec(memory_space=pltpu.SMEM)] + [any_space] * 5,
        out_specs=vmem,
        scratch_shapes=[
            pltpu.VMEM((rows, width), BF16),
            pltpu.VMEM((2 * ny, 4, width // (2 * ny), width), BF16),
            pltpu.VMEM((nt, keys_dev, width), BF16),
            pltpu.VMEM((width // 128, keys // 2, 128), F32),
            pltpu.VMEM((slots, regions), jnp.int32),
            pltpu.VMEM((slots, regions), jnp.int32),
            pltpu.VMEM((width,), F32),
            pltpu.VMEM((2, slots, regions), jnp.int32),
            pltpu.VMEM((2, slots, regions), jnp.int32),
            pltpu.VMEM((keys_dev, width), F32),
            pltpu.VMEM((2, keys_dev, width), F32),
            pltpu.VMEM((2, keys_dev, width), F32),
            pltpu.VMEM((2, HEADS // 2, 256, rows), BF16),
            pltpu.VMEM((2, keys // 4, width), BF16),
            pltpu.VMEM((2, width, keys // 4), BF16),
            pltpu.VMEM((width, rows), BF16),
            pltpu.VMEM((width, width), BF16),
            pltpu.VMEM((HEADS, 1, rows), F32),
            pltpu.VMEM((HEADS, 1, rows), F32),
            pltpu.VMEM((width, rows), F32),
            dma((8,)),
            dma((3, 2)),
            dma((3, 2)),
            dma((2,)),
            dma((2, 4)),
            dma((2, 4)),
            dma((2,)),
            dma((2,)),
            dma,
            dma((nz,)),
            dma,
            dma((2,)),
            pltpu.SemaphoreType.REGULAR((nz,)),
        ],
        compiler_params=pltpu.CompilerParams(
            collective_id=0, has_side_effects=True, vmem_limit_bytes=24 * 1024 * 1024
        ),
        name="dilated_attention",
    )(*(keep(a) for a in (tiles[0], idx, msk)), tile_count, *(keep(a) for a in (w_query, w_key, w_value, w_out, key_gain)))
    return out[None]


def solution(mesh, nz=NZ):
    ny = mesh.shape["fsdp"] // 2
    nx = mesh.shape["tile"] // nz
    placed = (
        P("fsdp", "tile", None),
        P("fsdp", "tile", None),
        P("fsdp", "tile", None),
        P("fsdp"),
        P("fsdp", None),
        P("fsdp", None),
        P("fsdp", None),
        P("fsdp", None),
        P(),
    )
    return jax.shard_map(
        functools.partial(body, ny, nx, nz),
        mesh=mesh, in_specs=placed, out_specs=P("fsdp", "tile", None), check_vma=False,
    )
```
